32 devices in a mesh: dp: 16 (over z, y, x), mp: 2 (over core).
Axes of the slice: x: 2, y: 2, z: 4, core: 2. Of those that a mesh axis runs over, the one named last changes fastest.
Arguments:
- layer_entries: bfloat16 [2, 2048, 1024], P(None, 'dp'), may hold values from -6 to 6
- loss_sensitivity: bfloat16 [2, 2048, 1024], P(None, 'dp'), may hold values from -6 to 6
- occupied_counts: int32 [2, 16], P(None, 'dp'), may hold values from 32 to 128, as said below
- earlier_normalizer_gain: float32 [1024], replicated, may hold values from 0.5 to 1.5
- inflow_logits: float32 [1024, 16], replicated, may hold values from -6 to 0
- decay_logits: float32 [1024, 16], replicated, may hold values from -4 to 2
- channel_lifting: float32 [1024, 16], replicated, may hold values from -6 to 6
- channel_collapse: float32 [1024, 16], replicated, may hold values from -3 to 3
- direct_term_weight: float32 [1024], replicated, may hold values from 0.5 to 1.5
- content_projector: bfloat16 [1024, 2048], P('dp', 'mp'), may hold values from -0.1875 to 0.1875
- content_offset: float32 [2048], P('mp'), may hold values from -1.2 to 1.2
- common_projector: bfloat16 [1024, 128], P('dp'), may hold values from -0.1875 to 0.1875
- common_offset: float32 [128], replicated, may hold values from -1.2 to 1.2
- asking_gain: float32 [128], replicated, may hold values from -12 to 12
- asking_offset: float32 [128], replicated, may hold values from -6 to 6
- lookup_gain: float32 [128], replicated, may hold values from -12 to 12
- forget_gate_matrix: bfloat16 [1024, 2048], P('dp', 'mp'), may hold values from -0.1875 to 0.1875
- forget_gate_offset: float32 [2048], P('mp'), may hold values from -1.2 to 1.2
- renewal_gate_matrix: bfloat16 [1024, 1024], P('dp'), may hold values from -0.1875 to 0.1875
- renewal_gate_offset: float32 [1024], replicated, may hold values from -1.2 to 1.2
- candidate_matrix: bfloat16 [1024, 1024], P('dp'), may hold values from -0.1875 to 0.1875
- candidate_offset: float32 [1024], replicated, may hold values from -1.2 to 1.2
- attended_projector: bfloat16 [2048, 1024], P('mp', 'dp'), may hold values from -0.5 to 0.5
- later_normalizer_gain: float32 [1024], replicated, may hold values from 0.5 to 1.5
- hidden_layer_matrix: bfloat16 [1024, 4096], P('dp', 'mp'), may hold values from -0.1875 to 0.1875
- hidden_layer_offset: float32 [4096], P('mp'), may hold values from -1.2 to 1.2
- outward_layer_matrix: bfloat16 [4096, 1024], P('mp', 'dp'), may hold values from -0.09375 to 0.09375
- outward_layer_offset: float32 [1024], replicated, may hold values from -1.2 to 1.2
Outputs:
- outputs: bfloat16 [2, 2048, 1024], P(None, 'dp')
- grad_tokens: bfloat16 [2, 2048, 1024], P(None, 'dp')
- grad_prenorm: float32 [1024], replicated
- grad_alphas: float32 [1024, 16], replicated
- grad_deltas: float32 [1024, 16], replicated
- grad_expand: float32 [1024, 16], replicated
- grad_readout: float32 [1024, 16], replicated
- grad_omegas: float32 [1024], replicated
- grad_wvalue: float32 [1024, 2048], P('dp', 'mp')
- grad_bvalue: float32 [2048], P('mp')
- grad_wshared: float32 [1024, 128], P('dp')
- grad_bshared: float32 [128], replicated
- grad_qscale: float32 [128], replicated
- grad_qshift: float32 [128], replicated
- key_scale_gradient: float32 [128], replicated
- grad_wreset: float32 [1024, 2048], P('dp', 'mp')
- grad_breset: float32 [2048], P('mp')
- grad_wupdate: float32 [1024, 1024], P('dp')
- grad_bupdate: float32 [1024], replicated
- grad_whidden: float32 [1024, 1024], P('dp')
- grad_bhidden: float32 [1024], replicated
- grad_woutput: float32 [2048, 1024], P('mp', 'dp')
- grad_postnorm: float32 [1024], replicated
- grad_wffnin: float32 [1024, 4096], P('dp', 'mp')
- grad_bffnin: float32 [4096], P('mp')
- grad_wffnout: float32 [4096, 1024], P('mp', 'dp')
- grad_bffnout: float32 [1024], replicated
The draws below stay inside these ranges and needn't reach their ends.
Inputs may be any that keep to these rules, and one draw needn't show every extreme that they name: `occupied_counts`: a row's live tokens come first and the rest of its 128 slots are padding; some row is full.
All inputs are finite; a program needn't handle non-finite values.
Results may differ from the reference program's by a relative error of at most 0.04.
Values may be sent and summed in bfloat16 or wider, within the bound.
No kernel may reach another device: no remote copies, remote signals or barrier semaphores. Data moves between devices by JAX's collectives and lax.ppermute only.
A program may use at most 256 MiB of HBM per device.

```python
import jax
import jax.numpy as jnp
from jax import lax

D = 1024
COMMON_SPAN_DIM = 128
V = 2048
H = 16
FF = 4096
SPAN = 128
TOK_DEV = 128
MICRO = 2
TOKENS = 2048
N_DP = 16


def draw_occupied_counts(key, part):
    short_key = jax.random.fold_in(key, 11)
    whole_key = jax.random.fold_in(key, 12)
    short = jax.random.randint(short_key, (MICRO, N_DP), TOK_DEV // 4, TOK_DEV)
    whole = jax.random.randint(whole_key, (MICRO, N_DP), 0, 8)
    drawn = jnp.where(whole == 0, TOK_DEV, short)
    drawn = drawn.at[0, 0].set(TOK_DEV)
    drawn = drawn.at[MICRO - 1, N_DP - 1].set(TOK_DEV // 4)
    return drawn.astype(jnp.int32)


def block_scale(rng, shape, pieces, smallest, top_value):
    def one(axis_at, blocks):
        steps = jax.random.uniform(jax.random.fold_in(jax.random.fold_in(rng, 6), axis_at), (blocks,), jnp.float32, smallest / len(pieces), top_value / len(pieces))
        return jnp.repeat(jnp.exp(steps), shape[axis_at] // blocks).reshape((-1,) + (1,) * (len(shape) - axis_at - 1))

    level = one(*pieces[0])
    for cut in pieces[1:]:
        level = level * one(*cut)
    return level


def centred(stream_key, shape, scale, limit, split=(), held_as=jnp.bfloat16):
    values = scale * jax.random.normal(stream_key, shape, jnp.float32)
    if split:
        values = values * block_scale(stream_key, shape, split, -0.22, 0.18)
    return jnp.clip(values, -limit, limit).astype(held_as)


def setup_inputs(seed: int = 0) -> dict:
    splits = jax.random.split(jax.random.key(seed), 29)
    return {
        "layer_entries": centred(splits[0], (MICRO, TOKENS, D), 1.0, 6.0, ((1, 16),)),
        "loss_sensitivity": centred(splits[1], (MICRO, TOKENS, D), 1.0, 6.0, ((1, 16),)),
        "occupied_counts": draw_occupied_counts(jax.random.fold_in(splits[28], 71), 0),
        "earlier_normalizer_gain": jnp.clip(1.0 + 0.1 * jax.random.normal(splits[3], (D,), jnp.float32), 0.5, 1.5),
        "inflow_logits": jnp.clip(jax.random.uniform(splits[4], (D, H), jnp.float32, -6.0, 0.0), -6.0, 0.0),
        "decay_logits": jnp.clip(jax.random.uniform(splits[5], (D, H), jnp.float32, -4.0, 2.0), -4.0, 2.0),
        "channel_lifting": centred(splits[6], (D, H), 1.0, 6.0, (), jnp.float32),
        "channel_collapse": centred(splits[7], (D, H), 0.5, 3.0, (), jnp.float32),
        "direct_term_weight": jnp.clip(jax.random.uniform(splits[8], (D,), jnp.float32, 0.5, 1.5), 0.5, 1.5),
        "content_projector": centred(splits[9], (D, V), D ** -0.5, 0.1875, ((0, 16), (1, 2))),
        "content_offset": centred(splits[10], (V,), 0.2, 1.2, ((0, 2),), jnp.float32),
        "common_projector": centred(splits[11], (D, COMMON_SPAN_DIM), D ** -0.5, 0.1875, ((0, 16),)),
        "common_offset": centred(splits[12], (COMMON_SPAN_DIM,), 0.2, 1.2, (), jnp.float32),
        "asking_gain": centred(splits[13], (COMMON_SPAN_DIM,), 2.0, 12.0, (), jnp.float32),
        "asking_offset": centred(splits[14], (COMMON_SPAN_DIM,), 1.0, 6.0, (), jnp.float32),
        "lookup_gain": centred(splits[15], (COMMON_SPAN_DIM,), 2.0, 12.0, (), jnp.float32),
        "forget_gate_matrix": centred(splits[16], (D, V), D ** -0.5, 0.1875, ((0, 16), (1, 2))),
        "forget_gate_offset": centred(splits[17], (V,), 0.2, 1.2, ((0, 2),), jnp.float32),
        "renewal_gate_matrix": centred(splits[18], (D, D), D ** -0.5, 0.1875, ((0, 16),)),
        "renewal_gate_offset": centred(splits[19], (D,), 0.2, 1.2, (), jnp.float32),
        "candidate_matrix": centred(splits[20], (D, D), D ** -0.5, 0.1875, ((0, 16),)),
        "candidate_offset": centred(splits[21], (D,), 0.2, 1.2, (), jnp.float32),
        "attended_projector": centred(splits[22], (V, D), (V // 16) ** -0.5, 0.5, ((0, 2), (1, 16))),
        "later_normalizer_gain": jnp.clip(1.0 + 0.1 * jax.random.normal(splits[23], (D,), jnp.float32), 0.5, 1.5),
        "hidden_layer_matrix": centred(splits[24], (D, FF), D ** -0.5, 0.1875, ((0, 16), (1, 2))),
        "hidden_layer_offset": centred(splits[25], (FF,), 0.2, 1.2, ((0, 2),), jnp.float32),
        "outward_layer_matrix": centred(splits[26], (FF, D), FF ** -0.5, 0.09375, ((0, 2), (1, 16))),
        "outward_layer_offset": centred(splits[27], (D,), 0.2, 1.2, (), jnp.float32),
    }


@jax.custom_vjp
def low(v):
    return lax.optimization_barrier(v.astype(jnp.bfloat16)).astype(jnp.float32)

@jax.custom_vjp
def low_back(v):
    return v

def low_keep(v):
    return (low(v), None)

def low_pass(kept, grad):
    return (grad,)

def back_keep(v):
    return (v, None)

def back_low(kept, grad):
    return (low(grad),)
low.defvjp(low_keep, low_pass)
low_back.defvjp(back_keep, back_low)
epsilon = 1e-05
highest = lax.Precision.HIGHEST
group_rows = 8

def matmul(left, right):
    return jnp.dot(left, right, precision=highest, preferred_element_type=jnp.float32)

def layer_norm(values, gain):
    center = values - lax.optimization_barrier(jnp.mean(values, axis=-1, keepdims=True))
    spread = lax.optimization_barrier(jnp.mean(center * center, axis=-1, keepdims=True))
    return center * lax.rsqrt(spread + epsilon) * gain

def ema_scan(normed, inflow_logits, decay_logits, channel_lifting, channel_collapse):
    rate_in = jax.nn.sigmoid(inflow_logits)
    keep_rate = 1.0 - rate_in * jax.nn.sigmoid(decay_logits)
    inflow = rate_in * channel_lifting

    def advance(state, column):
        state = keep_rate * state + inflow * column[:, :, None]
        return (state, lax.optimization_barrier(jnp.sum(channel_collapse * state, axis=-1)))
    start = jnp.zeros((normed.shape[0],) + inflow_logits.shape, normed.dtype)
    final_state, outputs = lax.scan(advance, start, jnp.swapaxes(normed, 0, 1))
    return jnp.swapaxes(outputs, 0, 1)

def forward_group(learnable_nested, inputs, live):
    earlier_normalizer_gain, inflow_logits, decay_logits, channel_lifting, channel_collapse, direct_term_weight, content_projector, content_offset, common_projector, common_offset, asking_gain, asking_offset, lookup_gain, forget_gate_matrix, forget_gate_offset, renewal_gate_matrix, renewal_gate_offset, candidate_matrix, candidate_offset, attended_projector, later_normalizer_gain, hidden_layer_matrix, hidden_layer_offset, outward_layer_matrix, outward_layer_offset = learnable_nested
    groups = inputs.shape[0]
    steps = inputs.shape[1]
    total = groups * steps
    normed = layer_norm(inputs, earlier_normalizer_gain)
    smooth = jax.nn.silu(ema_scan(normed, inflow_logits, decay_logits, channel_lifting, channel_collapse) + direct_term_weight * normed)
    norm_low = low(normed.reshape(total, D))
    smooth_low = low(smooth.reshape(total, D))
    value_pre = low_back(matmul(norm_low, content_projector) + content_offset)
    value_low = low(jax.nn.silu(value_pre))
    common_linear_sum = low_back(matmul(smooth_low, common_projector) + common_offset)
    common_embedding = jax.nn.silu(common_linear_sum)
    query_low = low(common_embedding * asking_gain + asking_offset)
    lookup_lowbit = low(common_embedding * lookup_gain)
    reset = jax.nn.silu(low_back(matmul(smooth_low, forget_gate_matrix) + forget_gate_offset))
    update = jax.nn.sigmoid(low_back(matmul(smooth_low, renewal_gate_matrix) + renewal_gate_offset))
    hidden_in = matmul(smooth_low, candidate_matrix) + candidate_offset
    blocks = total // SPAN
    query_blocks = query_low.reshape(blocks, SPAN, COMMON_SPAN_DIM)
    key_blocks = lookup_lowbit.reshape(blocks, SPAN, COMMON_SPAN_DIM)
    value_blocks = value_low.reshape(blocks, SPAN, V)
    position = jnp.arange(SPAN)
    live_blocks = live.reshape(blocks, SPAN)
    causal = position[None, :] <= position[:, None]
    diagonal = position[None, :] == position[:, None]
    allowed = causal[None] & ((live_blocks[:, None, :] == 1) | diagonal[None])
    raw_scores = jnp.einsum('ctz,csz->cts', query_blocks, key_blocks, precision=highest) * COMMON_SPAN_DIM ** (-0.5)
    scores = low_back(jnp.where(allowed, raw_scores, -1e+30))
    probs = low(jax.nn.softmax(scores, axis=-1))
    attended = low_back(jnp.einsum('cts,csv->ctv', probs, value_blocks, precision=highest)).reshape(total, V)
    mixed = low(reset * attended)
    hidden_pre = low_back(hidden_in + matmul(mixed, attended_projector))
    hidden = jax.nn.silu(hidden_pre)
    flat_in = inputs.reshape(total, D)
    blended = flat_in + update * (hidden - flat_in)
    ffn_low = low(layer_norm(blended, later_normalizer_gain))
    ffn_pre = low_back(matmul(ffn_low, hidden_layer_matrix) + hidden_layer_offset)
    ffn_act = low(jax.nn.silu(ffn_pre))
    ffn_out = low_back(matmul(ffn_act, outward_layer_matrix))
    live_float = live.reshape(total, 1).astype(inputs.dtype)
    result = live_float * (blended + ffn_out + outward_layer_offset)
    return result.reshape(groups, steps, D)

def reference(layer_entries, loss_sensitivity, occupied_counts, earlier_normalizer_gain, inflow_logits, decay_logits, channel_lifting, channel_collapse, direct_term_weight, content_projector, content_offset, common_projector, common_offset, asking_gain, asking_offset, lookup_gain, forget_gate_matrix, forget_gate_offset, renewal_gate_matrix, renewal_gate_offset, candidate_matrix, candidate_offset, attended_projector, later_normalizer_gain, hidden_layer_matrix, hidden_layer_offset, outward_layer_matrix, outward_layer_offset):
    learnable_nested = tuple((content_matrix.astype(jnp.float32) for content_matrix in (earlier_normalizer_gain, inflow_logits, decay_logits, channel_lifting, channel_collapse, direct_term_weight, content_projector, content_offset, common_projector, common_offset, asking_gain, asking_offset, lookup_gain, forget_gate_matrix, forget_gate_offset, renewal_gate_matrix, renewal_gate_offset, candidate_matrix, candidate_offset, attended_projector, later_normalizer_gain, hidden_layer_matrix, hidden_layer_offset, outward_layer_matrix, outward_layer_offset)))
    rows = MICRO * N_DP
    batches = rows // group_rows
    inputs = layer_entries.astype(jnp.float32).reshape(batches, group_rows, TOK_DEV, D)
    seeds = loss_sensitivity.astype(jnp.float32).reshape(batches, group_rows, TOK_DEV, D)
    flat_lengths = occupied_counts.reshape(rows).astype(jnp.int32)
    live = (jnp.arange(TOK_DEV).astype(jnp.int32)[None, :] < flat_lengths[:, None]).astype(jnp.int32)
    live = live.reshape(batches, group_rows, TOK_DEV)
    zeros = jax.tree.map(jnp.zeros_like, learnable_nested)

    def step(totals, item):
        group_in, group_seed, group_live = item
        result, pullback = jax.vjp(lambda weights, values: forward_group(weights, values, group_live), learnable_nested, group_in)
        weight_grads, input_grad = pullback(group_seed)
        totals = jax.tree.map(jnp.add, totals, weight_grads)
        return (totals, (result.astype(jnp.bfloat16), input_grad.astype(jnp.bfloat16)))
    totals, (results, input_grads) = lax.scan(step, zeros, (inputs, seeds, live))
    outputs = results.reshape(MICRO, N_DP * TOK_DEV, D)
    grad_tokens = input_grads.reshape(MICRO, N_DP * TOK_DEV, D)
    return (outputs, grad_tokens, totals[0], totals[1], totals[2], totals[3], totals[4], totals[5], totals[6], totals[7], totals[8], totals[9], totals[10], totals[11], totals[12], totals[13], totals[14], totals[15], totals[16], totals[17], totals[18], totals[19], totals[20], totals[21], totals[22], totals[23], totals[24])
```

```python
import functools

import jax
import jax.numpy as jnp
from jax import lax
from jax.experimental import pallas as pl
from jax.experimental.pallas import tpu as pltpu
from jax.sharding import PartitionSpec as P

COMMON_SPAN_DIM = 128
SPAN = 128
LANES = 128
SUBLANES = 8

epsilon = 1e-05
bf16 = jnp.bfloat16
f32 = jnp.float32


def product(left, right):
    return jnp.dot(left, right, preferred_element_type=f32)


def left_inner(left, right):
    return lax.dot_general(left, right, (((0,), (0,)), ((), ())), preferred_element_type=f32)


def right_inner(left, right):
    return lax.dot_general(left, right, (((1,), (1,)), ((), ())), preferred_element_type=f32)


def silu_slope(values):
    sigma = jax.nn.sigmoid(values)
    return sigma * (1.0 + values * (1.0 - sigma))


def radices_of(n):
    found = []
    while n > 1:
        r = 4 if n % 4 == 0 and (n > 4 or not found) else 2
        if n % r:
            r = n
        found.append(r)
        n //= r
    while len(found) < 3:
        found.append(1)
    return tuple(found)


class Grid:
    def __init__(self, n):
        self.n = n
        self.radix = radices_of(n)
        strides, left = [], n
        for r in self.radix:
            left //= r
            strides.append(left)
        self.stride = tuple(strides)

    def coords(self, index):
        return [(index // s) % r for s, r in zip(self.stride, self.radix)]

    def shift(self, dim, k):
        pairs = []
        for source in range(self.n):
            at = (source // self.stride[dim]) % self.radix[dim]
            to = (at + k) % self.radix[dim]
            pairs.append((source, source + (to - at) * self.stride[dim]))
        return pairs

    def gather_dim(self, array, dim):
        r = self.radix[dim]
        if r == 1:
            return array
        got = [array]
        for k in range(1, r):
            got.append(lax.ppermute(array, "dp", self.shift(dim, -k)))
        return jnp.concatenate(got, axis=dim)

    def scatter_dim(self, array, dim, last):
        r = self.radix[dim]
        if r == 1:
            return array.astype(f32) if last else array
        parts = [lax.slice_in_dim(array, k, k + 1, axis=dim) for k in range(r)]
        got = [parts[0]]
        for k in range(1, r):
            got.append(lax.ppermute(parts[k], "dp", self.shift(dim, k)))
        total = got[0].astype(f32)
        for g in got[1:]:
            total = total + g.astype(f32)
        return total if last else total.astype(bf16)

    def sum_all(self, value):
        for dim, r in reversed(list(enumerate(self.radix))):
            got = [value] + [
                lax.ppermute(value, "dp", self.shift(dim, -k)) for k in range(1, r)
            ]
            if r == 4:
                value = (got[0] + got[2]) + (got[1] + got[3])
            elif r == 2:
                value = got[0] + got[1]
            elif r > 2:
                value = lax.psum(value, "dp", axis_index_groups=self.groups(dim))
        return value

    def groups(self, dim):
        lines = {}
        for i in range(self.n):
            c = self.coords(i)
            c[dim] = 0
            lines.setdefault(tuple(c), []).append(i)
        return list(lines.values())

    def blocks(self, rows):
        return tuple(self.radix) + (rows,)

    def permutation(self, width):
        rows = width // self.n
        me = lax.axis_index("dp")
        place = jnp.arange(width)
        block = place // rows
        absolute = place % rows
        for s, r in zip(self.stride, self.radix):
            absolute = absolute + (((block // s) % r + (me // s) % r) % r) * (s * rows)
        return (jnp.arange(width)[:, None] == absolute[None, :]).astype(bf16)


def gather_all(grid, units, orders):
    done = []
    before = None
    for unit, order in zip(units, orders):
        rows, columns = unit.shape
        array = unit.reshape((1,) * len(grid.radix) + (rows, columns))
        if before is not None:
            array, before = lax.optimization_barrier((array, before))
            done[-1] = before
        array = grid.gather_dim(array, order[0])
        before = array
        done.append(array)
    full = []
    for array, order in zip(done, orders):
        for dim in order[1:]:
            array = grid.gather_dim(array, dim)
        full.append(array.reshape(grid.n * array.shape[-2], array.shape[-1]))
    return full


def scatter_one(grid, array, order):
    total, columns = array.shape
    rows = total // grid.n
    array = array.astype(bf16).reshape(grid.blocks(rows) + (columns,))
    for at, dim in enumerate(order):
        array = grid.scatter_dim(array, dim, at == len(order) - 1)
    return array.reshape(rows, columns)


def tiles_of(array):
    return [array[i * SUBLANES : (i + 1) * SUBLANES] for i in range(array.shape[0] // SUBLANES)]


def row_tile(table_ref, lag, c):
    row = table_ref[lag, pl.ds(c, 1), :]
    return jnp.broadcast_to(row, (SUBLANES, LANES))


def norm_parts(x_ref):
    values = x_ref[...].astype(f32)
    center = values - jnp.mean(values, axis=-1, keepdims=True)
    scale = lax.rsqrt(jnp.mean(center * center, axis=-1, keepdims=True) + epsilon)
    return center * scale, scale


def ema_forward_kernel(
    x_ref, gain_ref, direct_ref, inflow_ref, decay_ref, lift_ref, collapse_ref,
    normed_ref, pre_ref, norm_low_ref, smooth_low_ref, table_ref,
):
    steps = x_ref.shape[0]
    hat, unused = norm_parts(x_ref)
    normed = hat * gain_ref[...]
    normed_ref[...] = normed
    norm_low_ref[...] = normed.astype(bf16)
    rate = jax.nn.sigmoid(inflow_ref[...])
    keep = 1.0 - rate * jax.nn.sigmoid(decay_ref[...])
    weight = collapse_ref[...] * (rate * lift_ref[...])

    def lag_step(lag, power):
        table_ref[lag] = jnp.sum(weight * power, axis=0)
        return power * keep

    lax.fori_loop(0, steps, lag_step, jnp.ones_like(keep))
    count = steps // SUBLANES
    sub = lax.broadcasted_iota(jnp.int32, (steps, LANES), 0)

    def block(c, carry):
        columns = pl.ds(pl.multiple_of(c * LANES, LANES), LANES)
        base = normed_ref[:, columns]
        total = [jnp.zeros((SUBLANES, LANES), f32)] * count
        for r in range(SUBLANES):
            moved = base if r == 0 else jnp.where(sub >= r, pltpu.roll(base, r, 0), 0.0)
            moved = tiles_of(moved)
            for q in range(count):
                w = row_tile(table_ref, q * SUBLANES + r, c)
                for i in range(q, count):
                    total[i] = total[i] + w * moved[i - q]
        pre = jnp.concatenate(total, axis=0) + direct_ref[:, columns] * base
        pre_ref[:, columns] = pre
        smooth_low_ref[:, columns] = (pre * jax.nn.sigmoid(pre)).astype(bf16)
        return carry

    lax.fori_loop(0, x_ref.shape[1] // LANES, block, 0)


def ema_backward_kernel(
    x_ref, gain_ref, direct_ref, inflow_ref, decay_ref, table_ref, normed_ref, pre_ref,
    grad_smooth_ref, grad_normed_ref, grad_input_ref,
    grad_row_ref, vectors_ref, zero_ref, first_ref,
    inner_ref, lag_ref,
):
    steps = x_ref.shape[0]
    count = steps // SUBLANES
    sub = lax.broadcasted_iota(jnp.int32, (steps, LANES), 0)

    def block(c, carry):
        columns = pl.ds(pl.multiple_of(c * LANES, LANES), LANES)
        pre = pre_ref[:, columns]
        grad_pre = grad_smooth_ref[:, columns] * silu_slope(pre)
        normed = normed_ref[:, columns]
        vectors_ref[1:2, columns] = jnp.sum(grad_pre * normed, axis=0, keepdims=True)
        own = tiles_of(normed)
        total = tiles_of(grad_normed_ref[:, columns] + direct_ref[:, columns] * grad_pre)
        for r in range(SUBLANES):
            moved = grad_pre
            if r:
                moved = jnp.where(sub < steps - r, pltpu.roll(grad_pre, steps - r, 0), 0.0)
            moved = tiles_of(moved)
            for q in range(count):
                w = row_tile(table_ref, q * SUBLANES + r, c)
                lag_sum = jnp.zeros((SUBLANES, LANES), f32)
                for i in range(count - q):
                    g = moved[i + q]
                    total[i] = total[i] + w * g
                    lag_sum = lag_sum + g * own[i]
                lag_ref[q * SUBLANES + r, pl.ds(c, 1), :] = jnp.sum(lag_sum, axis=0, keepdims=True)
        inner_ref[:, columns] = jnp.concatenate(total, axis=0)
        return carry

    lax.fori_loop(0, x_ref.shape[1] // LANES, block, 0)

    keep_all = 1.0 - jax.nn.sigmoid(inflow_ref[...]) * jax.nn.sigmoid(decay_ref[...])
    half = keep_all.shape[0] // 2
    for h in range(2):
        keep = keep_all[h * half : (h + 1) * half]

        def lag_step(lag, carry):
            power, zero, first = carry
            g = lag_ref[lag]
            first = first + (g * lag.astype(f32))[None] * power
            power = power * keep
            return (power, zero + g[None] * power, first)

        blank = jnp.zeros_like(keep)
        start = (jnp.ones_like(keep), blank + lag_ref[0][None], blank)
        unused, zero, first = lax.fori_loop(1, steps, lag_step, start)
        zero_ref[h * half : (h + 1) * half] = zero
        first_ref[h * half : (h + 1) * half] = first

    hat, scale = norm_parts(x_ref)
    grad = inner_ref[...]
    vectors_ref[0:1] = jnp.sum(grad * hat, axis=0, keepdims=True)
    grad = grad * gain_ref[...]
    grad = grad - jnp.mean(grad, axis=-1, keepdims=True) - hat * jnp.mean(
        grad * hat, axis=-1, keepdims=True
    )
    grad_row_ref[...] = (grad_input_ref[...] + scale * grad).astype(bf16)


def ema_forward(x, gain, direct, folded):
    steps, width = x.shape
    like = jax.ShapeDtypeStruct
    return pl.pallas_call(
        ema_forward_kernel,
        name="average_forward",
        out_shape=(
            like((steps, width), f32),
            like((steps, width), f32),
            like((steps, width), bf16),
            like((steps, width), bf16),
            like((steps, width // LANES, LANES), f32),
        ),
        cost_estimate=pl.CostEstimate(flops=20_000_000, bytes_accessed=3_000_000, transcendentals=0),
    )(x, gain[None], direct[None], *folded)


def ema_backward(x, gain, direct, folded, table, normed, pre, grad_smooth, grad_normed, grad_input):
    steps, width = x.shape
    like = jax.ShapeDtypeStruct
    inflow, decay = folded[0], folded[1]
    return pl.pallas_call(
        ema_backward_kernel,
        name="average_backward",
        out_shape=(
            like((steps, width), bf16),
            like((2, width), f32),
            like(inflow.shape, f32),
            like(inflow.shape, f32),
        ),
        scratch_shapes=[
            pltpu.VMEM((steps, width), f32),
            pltpu.VMEM((steps, width // LANES, LANES), f32),
        ],
        cost_estimate=pl.CostEstimate(flops=40_000_000, bytes_accessed=4_000_000, transcendentals=0),
    )(x, gain[None], direct[None], inflow, decay, table, normed, pre, grad_smooth, grad_normed, grad_input)


def per_device(
    grid,
    layer_entries,
    loss_sensitivity,
    occupied_counts,
    earlier_normalizer_gain,
    inflow_logits,
    decay_logits,
    channel_lifting,
    channel_collapse,
    direct_term_weight,
    content_projector,
    content_offset,
    common_projector,
    common_offset,
    asking_gain,
    asking_offset,
    lookup_gain,
    forget_gate_matrix,
    forget_gate_offset,
    renewal_gate_matrix,
    renewal_gate_offset,
    candidate_matrix,
    candidate_offset,
    attended_projector,
    later_normalizer_gain,
    hidden_layer_matrix,
    hidden_layer_offset,
    outward_layer_matrix,
    outward_layer_offset,
):
    core = lax.axis_index("mp")
    micro, steps, width = layer_entries.shape
    half = width // 2
    swap_pairs = [(0, 1), (1, 0)]

    def swap(value):
        return lax.ppermute(value, "mp", swap_pairs)

    def both(own):
        return jnp.concatenate([own, swap(own)], axis=0)

    def reduce_rows(part, send=f32):
        return part[:steps] + swap(part[steps:].astype(send)).astype(f32)

    def in_order(own, other, axis):
        first = jnp.where(core == 0, own, other)
        second = jnp.where(core == 0, other, own)
        return jnp.concatenate([first, second], axis=axis)

    def half_of(value, which, axis):
        return lax.dynamic_slice_in_dim(value, which * half, half, axis=axis)

    ff = hidden_layer_matrix.shape[1] // 2
    misc = jnp.concatenate(
        [
            half_of(renewal_gate_matrix, core, 1),
            half_of(candidate_matrix, core, 1),
            common_projector,
        ],
        axis=1,
    )
    outward_t = outward_layer_matrix.T
    units = [
        content_projector,
        misc,
        forget_gate_matrix,
        attended_projector.T,
        hidden_layer_matrix[:, :ff],
        outward_t[:, :ff],
        hidden_layer_matrix[:, ff:],
        outward_t[:, ff:],
    ]
    dims = list(range(len(grid.radix)))
    alpha = [0] + dims[:0:-1]
    beta = dims
    orders = [alpha, beta] * 4
    (w_value, w_misc, w_reset, w_out, w_in_a, w_down_a, w_in_b, w_down_b) = gather_all(
        grid, units, orders
    )
    w_gates, w_shared = w_misc[:, : 2 * half], w_misc[:, 2 * half :]

    row_in = lax.dynamic_index_in_dim(layer_entries, core, 0, keepdims=False)
    row_seed = lax.dynamic_index_in_dim(loss_sensitivity, core, 0, keepdims=False)
    lengths = jnp.stack(
        [
            lax.dynamic_index_in_dim(occupied_counts[:, 0], core, 0, keepdims=False),
            lax.dynamic_index_in_dim(occupied_counts[:, 0], 1 - core, 0, keepdims=False),
        ]
    )
    position = jnp.arange(steps)
    live_rows = position[None, :] < lengths[:, None]
    live = live_rows[0].astype(f32)[:, None]
    spread = grid.permutation(width)

    def relative(value):
        return product(value, spread).astype(bf16)

    def absolute(value):
        return lax.dot_general(
            value,
            spread.astype(f32),
            (((1,), (1,)), ((), ())),
            precision=lax.Precision.HIGHEST,
            preferred_element_type=f32,
        )

    def fold(value):
        return value.T.reshape(value.shape[1], width // LANES, LANES)

    folded = [fold(v) for v in (inflow_logits, decay_logits, channel_lifting, channel_collapse)]
    seed = live * row_seed.astype(f32)
    seed2 = both(relative(seed.astype(bf16)))
    normed, pre, norm_low, smooth_low, table = ema_forward(
        row_in, earlier_normalizer_gain, direct_term_weight, folded
    )
    norm2 = both(relative(norm_low))
    smooth2 = both(relative(smooth_low))
    input_full = row_in.astype(f32)

    value_pre = product(norm2, w_value) + content_offset
    value_low = jax.nn.silu(value_pre).astype(bf16)
    shared_pre = product(smooth2, w_shared) + common_offset
    shared = jax.nn.silu(shared_pre)
    query_low = (shared * asking_gain + asking_offset).astype(bf16)
    key_low = (shared * lookup_gain).astype(bf16)
    reset_pre = product(smooth2, w_reset) + forget_gate_offset
    reset = jax.nn.silu(reset_pre)
    gates = product(smooth2, w_gates)
    gates_other = swap(gates[steps:])
    update = jax.nn.sigmoid(
        in_order(gates[:steps, :half], gates_other[:, :half], 1) + renewal_gate_offset
    )
    hidden_in = in_order(gates[:steps, half:], gates_other[:, half:], 1) + candidate_offset
    query_rows = query_low.reshape(micro, SPAN, -1)
    key_rows = key_low.reshape(micro, SPAN, -1)
    value_rows = value_low.reshape(micro, SPAN, -1)
    causal = position[None, :] <= position[:, None]
    diagonal = position[None, :] == position[:, None]
    allowed = causal[None] & (live_rows[:, None, :] | diagonal[None])
    scale = COMMON_SPAN_DIM ** (-0.5)
    raw_scores = jnp.einsum("ctz,csz->cts", query_rows, key_rows, preferred_element_type=f32)
    probs = jax.nn.softmax(jnp.where(allowed, raw_scores * scale, -1e30), axis=-1)
    probs_low = probs.astype(bf16)
    attended = jnp.einsum(
        "cts,csv->ctv", probs_low, value_rows, preferred_element_type=f32
    ).reshape(micro * steps, -1)
    mixed = (reset * attended).astype(bf16)
    hidden_pre = hidden_in + absolute(reduce_rows(right_inner(mixed, w_out)))
    hidden = jax.nn.silu(hidden_pre)
    blended = input_full + update * (hidden - input_full)
    center = blended - jnp.mean(blended, axis=-1, keepdims=True)
    post_scale = lax.rsqrt(jnp.mean(center * center, axis=-1, keepdims=True) + epsilon)
    hat = center * post_scale
    ffn2 = both(relative((hat * later_normalizer_gain).astype(bf16)))

    down_part = None
    ffn_norm_part = None
    ffn_grads = []
    bffnin = []
    for at, (w_in, w_down) in enumerate(((w_in_a, w_down_a), (w_in_b, w_down_b))):
        ffn_pre = product(ffn2, w_in) + hidden_layer_offset[at * ff : (at + 1) * ff]
        act = jax.nn.silu(ffn_pre).astype(bf16)
        grad_pre = (product(seed2, w_down) * silu_slope(ffn_pre)).astype(bf16)
        bffnin.append(jnp.sum(grad_pre.astype(f32), axis=0))
        down = right_inner(act, w_down)
        back = right_inner(grad_pre, w_in)
        down_part = down if down_part is None else down_part + down
        ffn_norm_part = back if ffn_norm_part is None else ffn_norm_part + back
        ffn_grads.append(left_inner(ffn2, grad_pre))
        ffn_grads.append(left_inner(seed2, act))
    scatter_orders = [alpha[::-1], beta[::-1]]
    ffn_out = [scatter_one(grid, g, scatter_orders[i % 2]) for i, g in enumerate(ffn_grads)]

    down_full = absolute(reduce_rows(down_part, bf16))
    out_row = (live * (blended + down_full + outward_layer_offset)).astype(bf16)

    grad_ffn_norm = absolute(reduce_rows(ffn_norm_part))
    grad_postnorm = jnp.sum(grad_ffn_norm * hat, axis=0)
    grad_hat = grad_ffn_norm * later_normalizer_gain
    grad_blended = seed + post_scale * (
        grad_hat
        - jnp.mean(grad_hat, axis=-1, keepdims=True)
        - hat * jnp.mean(grad_hat * hat, axis=-1, keepdims=True)
    )
    grad_input = grad_blended * (1.0 - update)
    grad_hidden = (grad_blended * update * silu_slope(hidden_pre)).astype(bf16)
    grad_update = (grad_blended * (hidden - input_full) * update * (1.0 - update)).astype(bf16)
    grad_hidden2 = both(relative(grad_hidden))
    mine = jnp.concatenate([half_of(grad_update, core, 1), half_of(grad_hidden, core, 1)], axis=1)
    theirs = jnp.concatenate(
        [half_of(grad_update, 1 - core, 1), half_of(grad_hidden, 1 - core, 1)], axis=1
    )
    grad_gates2 = jnp.concatenate([mine, swap(theirs)], axis=0)

    grad_mixed = product(grad_hidden2, w_out)
    grad_attended = (grad_mixed * reset).astype(bf16)
    grad_reset = (grad_mixed * attended * silu_slope(reset_pre)).astype(bf16)
    grad_att_rows = grad_attended.reshape(micro, SPAN, -1)
    probs_part = jnp.einsum(
        "ctv,csv->cts", grad_att_rows, value_rows, preferred_element_type=f32
    )
    theirs_part = swap(probs_part)
    grad_probs = probs_part + jnp.concatenate([theirs_part[1:], theirs_part[:1]], axis=0)
    grad_value = jnp.einsum(
        "cts,ctv->csv", probs_low, grad_att_rows, preferred_element_type=f32
    ).reshape(micro * steps, -1)
    grad_value_pre = (grad_value * silu_slope(value_pre)).astype(bf16)
    own_probs, own_grad = probs[0], grad_probs[0]
    grad_scores = (
        own_probs * (own_grad - jnp.sum(own_grad * own_probs, axis=-1, keepdims=True))
    ).astype(bf16)
    grad_query = product(grad_scores, key_rows[0]) * scale
    grad_key = left_inner(grad_scores, query_rows[0]) * scale
    own_shared = shared[:steps]
    grad_shared = (
        (grad_query * asking_gain + grad_key * lookup_gain) * silu_slope(shared_pre[:steps])
    ).astype(bf16)
    grad_misc = jnp.concatenate(
        [grad_gates2, jnp.concatenate([grad_shared, jnp.zeros_like(grad_shared)], axis=0)], axis=1
    )
    smooth_part = right_inner(grad_reset, w_reset) + right_inner(grad_misc, w_misc)
    norm_part = right_inner(grad_value_pre, w_value)
    grad_both = absolute(
        jnp.concatenate([reduce_rows(smooth_part, bf16), reduce_rows(norm_part, bf16)], axis=0)
    )
    grad_row, grad_vectors, grad_zero, grad_first = ema_backward(
        row_in,
        earlier_normalizer_gain,
        direct_term_weight,
        folded,
        table,
        normed,
        pre,
        grad_both[:steps],
        grad_both[steps:],
        grad_input,
    )
    out_wout = scatter_one(grid, left_inner(grad_hidden2, mixed), scatter_orders[1])
    out_reset = scatter_one(grid, left_inner(smooth2, grad_reset), scatter_orders[0])
    out_value = scatter_one(grid, left_inner(norm2, grad_value_pre), scatter_orders[0])
    out_misc = scatter_one(grid, left_inner(smooth2, grad_misc), scatter_orders[1])

    lanes = COMMON_SPAN_DIM
    narrow = jnp.concatenate(
        [
            jnp.sum(grad_shared.astype(f32), axis=0),
            jnp.sum(grad_query * own_shared, axis=0),
            jnp.sum(grad_query, axis=0),
            jnp.sum(grad_key * own_shared, axis=0),
        ]
    )
    narrow = jnp.pad(narrow, (0, width - 4 * lanes))[None]
    states = grad_zero.shape[0]
    shared_sums = jnp.concatenate(
        [
            grad_zero.reshape(states, width),
            grad_first.reshape(states, width),
            grad_vectors,
            jnp.sum(grad_update.astype(f32), axis=0)[None],
            jnp.sum(grad_hidden.astype(f32), axis=0)[None],
            grad_postnorm[None],
            jnp.sum(seed, axis=0)[None],
            narrow,
            jnp.zeros((1, width), f32),
        ],
        axis=0,
    )
    rows = shared_sums.shape[0] // 2
    keep_rows = lax.dynamic_slice_in_dim(shared_sums, core * rows, rows, axis=0)
    send_rows = lax.dynamic_slice_in_dim(shared_sums, (1 - core) * rows, rows, axis=0)
    keep_rows = keep_rows + swap(send_rows)
    wide_sums = jnp.concatenate(
        [
            jnp.sum(grad_value_pre.astype(f32), axis=0)[None],
            jnp.sum(grad_reset.astype(f32), axis=0)[None],
            bffnin[0].reshape(-1, width),
            bffnin[1].reshape(-1, width),
        ],
        axis=0,
    )
    sums = grid.sum_all(jnp.concatenate([keep_rows, wide_sums], axis=0))
    first_rows = sums[:rows]
    whole = in_order(first_rows, swap(first_rows), 0)
    wide = sums[rows:]
    zero = whole[:states].T
    first = whole[states : 2 * states].T
    rate = jax.nn.sigmoid(inflow_logits)
    damp = jax.nn.sigmoid(decay_logits)
    grad_collapse = rate * channel_lifting * zero
    grad_inflow = channel_collapse * zero
    grad_keep = channel_collapse * rate * channel_lifting * first
    grad_lifting = grad_inflow * rate
    grad_rate = (grad_inflow * channel_lifting - grad_keep * damp) * rate * (1.0 - rate)
    grad_damp = -grad_keep * rate * damp * (1.0 - damp)
    rest = whole[2 * states :]
    thin = rest[6].reshape(-1, lanes)

    gates_half = out_misc[:, : 2 * half]
    gates_full_other = swap(gates_half)
    out_update = in_order(gates_half[:, :half], gates_full_other[:, :half], 1)
    out_hidden = in_order(gates_half[:, half:], gates_full_other[:, half:], 1)
    out_shared = out_misc[:, 2 * half :]
    out_shared = out_shared + swap(out_shared)

    rows_out = jnp.stack([out_row, grad_row])
    rows_other = swap(rows_out)
    outputs = in_order(rows_out[:1], rows_other[:1], 0)
    grad_tokens = in_order(rows_out[1:], rows_other[1:], 0)
    return (
        outputs,
        grad_tokens,
        rest[0],
        grad_rate,
        grad_damp,
        grad_lifting,
        grad_collapse,
        rest[1],
        out_value,
        wide[0],
        out_shared,
        thin[0],
        thin[1],
        thin[2],
        thin[3],
        out_reset,
        wide[1],
        out_update,
        rest[2],
        out_hidden,
        rest[3],
        out_wout.T,
        rest[4],
        jnp.concatenate([ffn_out[0], ffn_out[2]], axis=1),
        wide[2:].reshape(-1),
        jnp.concatenate([ffn_out[1].T, ffn_out[3].T], axis=0),
        rest[5],
    )


def solution(mesh):
    grid = Grid(mesh.shape["dp"])
    return jax.shard_map(
        functools.partial(per_device, grid),
        mesh=mesh,
        in_specs=(
            P(None, "dp", None),
            P(None, "dp", None),
            P(None, "dp"),
            P(),
            P(),
            P(),
            P(),
            P(),
            P(),
            P("dp", "mp"),
            P("mp"),
            P("dp", None),
            P(),
            P(),
            P(),
            P(),
            P("dp", "mp"),
            P("mp"),
            P("dp", None),
            P(),
            P("dp", None),
            P(),
            P("mp", "dp"),
            P(),
            P("dp", "mp"),
            P("mp"),
            P("mp", "dp"),
            P(),
        ),
        out_specs=(
            P(None, "dp", None),
            P(None, "dp", None),
            P(),
            P(),
            P(),
            P(),
            P(),
            P(),
            P("dp", "mp"),
            P("mp"),
            P("dp", None),
            P(),
            P(),
            P(),
            P(),
            P("dp", "mp"),
            P("mp"),
            P("dp", None),
            P(),
            P("dp", None),
            P(),
            P("mp", "dp"),
            P(),
            P("dp", "mp"),
            P("mp"),
            P("mp", "dp"),
            P(),
        ),
        check_vma=False,
    )
```

```python
import functools

import jax
import jax.numpy as jnp
from jax import lax
from jax.experimental import pallas as pl
from jax.experimental.pallas import tpu as pltpu
from jax.sharding import PartitionSpec as P

COMMON_SPAN_DIM = 128
SPAN = 128
LANES = 128
SUBLANES = 8

epsilon = 1e-05
bf16 = jnp.bfloat16
f32 = jnp.float32


def product(left, right):
    return jnp.dot(left, right, preferred_element_type=f32)


def left_inner(left, right):
    return lax.dot_general(left, right, (((0,), (0,)), ((), ())), preferred_element_type=f32)


def right_inner(left, right):
    return lax.dot_general(left, right, (((1,), (1,)), ((), ())), preferred_element_type=f32)


def silu_slope(values):
    sigma = jax.nn.sigmoid(values)
    return sigma * (1.0 + values * (1.0 - sigma))


def radices_of(n):
    found = []
    left = n // 2
    while left > 1:
        r = 4 if left % 4 == 0 or not found and left > 4 else 2
        r = r if left % r == 0 else left
        found.append(r)
        left //= r
    while len(found) < 2:
        found.append(1)
    return tuple(found) + (2,)


class Grid:
    def __init__(self, n):
        self.n = n
        radix = radices_of(n)
        strides, left = [], n
        for r in radix:
            left //= r
            strides.append(left)
        self.radix = radix[1:-1] + radix[:1] + radix[-1:]
        self.stride = tuple(strides[1:-1] + strides[:1] + strides[-1:])
        self.near = len(radix) - 1
        self.line = len(radix) - 2

    def shift(self, dim, k):
        pairs = []
        for source in range(self.n):
            at = (source // self.stride[dim]) % self.radix[dim]
            to = (at + k) % self.radix[dim]
            pairs.append((source, source + (to - at) * self.stride[dim]))
        return pairs

    def fetch(self, array, dim):
        return [array] + [
            lax.ppermute(array, "dp", self.shift(dim, -k)) for k in range(1, self.radix[dim])
        ]

    def deliver(self, parts, dim):
        return [parts[0]] + [
            lax.ppermute(parts[k], "dp", self.shift(dim, k)) for k in range(1, self.radix[dim])
        ]

    def near_index(self):
        return lax.axis_index("dp") % 2

    def near_swap(self, value):
        return lax.ppermute(value, "dp", self.shift(self.near, 1))

    def sum_all(self, value):
        for dim, r in reversed(list(enumerate(self.radix))):
            got = self.fetch(value, dim)
            if r == 4:
                value = (got[0] + got[2]) + (got[1] + got[3])
            elif r == 2:
                value = got[0] + got[1]
            elif r > 2:
                value = lax.psum(value, "dp", axis_index_groups=self.groups(dim))
        return value

    def groups(self, dim):
        lines = {}
        for i in range(self.n):
            at = (i // self.stride[dim]) % self.radix[dim]
            lines.setdefault(i - at * self.stride[dim], []).append(i)
        return list(lines.values())

    def permutation(self, width):
        rows = width // self.n
        me = lax.axis_index("dp")
        place = jnp.arange(width)
        block = place // rows
        absolute = place % rows + (block % 2) * rows
        block = block // 2
        for s, r in list(zip(self.stride, self.radix))[-2::-1]:
            absolute = absolute + ((block % r + (me // s) % r) % r) * (s * rows)
            block = block // r
        return (jnp.arange(width)[:, None] == absolute[None, :]).astype(bf16)


def total_of(parts):
    total = parts[0].astype(f32)
    for p in parts[1:]:
        total = total + p.astype(f32)
    return total


def tie(values):
    return lax.optimization_barrier(values)


class Gather:
    def __init__(self, grid, mine, theirs):
        self.grid = grid
        near = grid.near_index()
        pack = functools.partial(jnp.concatenate, axis=1)
        kept = [pack(chunk) for chunk in mine]
        sent = [pack(chunk) for chunk in theirs]

        def beside(own, other):
            return jnp.stack([jnp.where(near == 0, own, other), jnp.where(near == 0, other, own)])

        first = beside(kept[0], grid.near_swap(sent[0]))
        rest = pack(sent[1:])
        first, rest = tie((first, rest))
        rest = grid.near_swap(rest)
        self.state, at = [first], 0
        for own in kept[1:]:
            self.state.append(beside(own, rest[:, at : at + own.shape[1]]))
            at += own.shape[1]
        self.middle = list(range(grid.line - 1, -1, -1))
        self.weights = {}
        self.stage = 0

    def advance(self, held=None):
        stage, count = self.stage, len(self.state)
        active = [k for k in range(count) if 0 <= stage - k <= len(self.middle)]
        last = stage - 1 - len(self.middle)
        done = self.weights[last] if last in self.weights else []
        if stage:
            tied, done, held = tie(([self.state[k] for k in active], done, held))
            for k, value in zip(active, tied):
                self.state[k] = value
            if last in self.weights:
                self.weights[last] = done
        for k in active:
            step = stage - k
            dim = self.grid.line if step == 0 else self.middle[step - 1]
            got = self.grid.fetch(self.state[k], dim)
            if step < len(self.middle):
                self.state[k] = jnp.stack(got)
            else:
                self.weights[k] = [g.reshape(-1, g.shape[-1]) for g in got]
        self.stage += 1
        return held

    def until(self, k):
        while k not in self.weights:
            self.advance()


class Moving:
    def __init__(self, grid, parts):
        self.grid = grid
        shape = grid.radix[1:] + (-1, parts[0].shape[-1])
        self.parts = [p.reshape(shape) for p in parts]
        self.value = None

    def across(self):
        self.value = total_of(self.grid.deliver(self.parts, 0))
        for dim in range(1, self.grid.line):
            value = self.value.astype(bf16)
            self.value = total_of(
                self.grid.deliver([value[k] for k in range(self.grid.radix[dim])], dim)
            )
        self.value = self.value.astype(bf16)

    def along(self):
        parts = [self.value[k] for k in range(self.grid.radix[self.grid.line])]
        self.value = total_of(self.grid.deliver(parts, self.grid.line))

    def near(self):
        near = self.grid.near_index()
        kept = lax.dynamic_index_in_dim(self.value, near, 0, keepdims=False)
        sent = lax.dynamic_index_in_dim(self.value, 1 - near, 0, keepdims=False)
        return kept, self.grid.near_swap(sent.astype(bf16)).astype(f32)


def tiles_of(array):
    return [array[i * SUBLANES : (i + 1) * SUBLANES] for i in range(array.shape[0] // SUBLANES)]


def row_tile(table_ref, lag, c):
    row = table_ref[lag, pl.ds(c, 1), :]
    return jnp.broadcast_to(row, (SUBLANES, LANES))


def norm_parts(x_ref):
    values = x_ref[...].astype(f32)
    center = values - jnp.mean(values, axis=-1, keepdims=True)
    scale = lax.rsqrt(jnp.mean(center * center, axis=-1, keepdims=True) + epsilon)
    return center * scale, scale


def sigma_of(values):
    return jax.nn.sigmoid(values)


def call(kernel, name, out, operands, scalars=0, scratch=()):
    specs = [pl.BlockSpec(memory_space=pltpu.SMEM)] * scalars
    specs += [pl.BlockSpec(memory_space=pltpu.VMEM)] * (len(operands) - scalars)
    return pl.pallas_call(
        kernel,
        name=name,
        out_shape=[jax.ShapeDtypeStruct(shape, dtype) for shape, dtype in out],
        in_specs=specs,
        out_specs=[pl.BlockSpec(memory_space=pltpu.VMEM)] * len(out),
        scratch_shapes=list(scratch),
        cost_estimate=pl.CostEstimate(flops=1, bytes_accessed=1, transcendentals=0),
    )(*operands)


def times(x, blocks, start, stop):
    total, at = None, 0
    for w in blocks:
        rows = w.shape[0]
        term = product(x[:, at : at + rows], w[:, start:stop])
        total = term if total is None else total + term
        at += rows
    return total


def times_t(x, blocks, start, stop):
    return jnp.concatenate([right_inner(x, w[:, start:stop]) for w in blocks], axis=1)


def to_absolute(value, spread):
    high = value.astype(bf16)
    low = (value - high.astype(f32)).astype(bf16)
    return right_inner(high, spread) + right_inner(low, spread)


def column_sum(values):
    return jnp.sum(values, axis=0, keepdims=True)


def ema_forward_kernel(
    place_ref, x_ref, seed_ref, gain_ref, direct_ref, params_ref, spread_ref,
    normed_ref, pre_ref, packed_ref, seed_low_ref, table_ref, seed_sum_ref,
):
    steps, width = x_ref.shape
    spread = spread_ref[...]
    hat, unused = norm_parts(x_ref)
    normed = hat * gain_ref[...]
    normed_ref[...] = normed
    packed_ref[:, width:] = product(normed.astype(bf16), spread).astype(bf16)
    live = lax.broadcasted_iota(jnp.int32, (steps, 1), 0) < place_ref[2]
    seed = jnp.where(live, seed_ref[...].astype(f32), 0.0)
    seed_sum_ref[...] = column_sum(seed)
    seed_low_ref[...] = product(seed.astype(bf16), spread).astype(bf16)
    rate = jax.nn.sigmoid(params_ref[0])
    keep = 1.0 - rate * jax.nn.sigmoid(params_ref[1])
    weight = params_ref[3] * (rate * params_ref[2])

    def lag_step(lag, power):
        table_ref[lag] = jnp.sum(weight * power, axis=0)
        return power * keep

    lax.fori_loop(0, steps, lag_step, jnp.ones_like(keep))
    count = steps // SUBLANES
    sub = lax.broadcasted_iota(jnp.int32, (steps, LANES), 0)

    def block(c, carry):
        columns = pl.ds(pl.multiple_of(c * LANES, LANES), LANES)
        base = normed_ref[:, columns]
        total = [jnp.zeros((SUBLANES, LANES), f32)] * count
        for r in range(SUBLANES):
            moved = base if r == 0 else jnp.where(sub >= r, pltpu.roll(base, r, 0), 0.0)
            moved = tiles_of(moved)
            for q in range(count):
                w = row_tile(table_ref, q * SUBLANES + r, c)
                for i in range(q, count):
                    total[i] = total[i] + w * moved[i - q]
        pre_ref[:, columns] = jnp.concatenate(total, axis=0) + direct_ref[:, columns] * base
        return carry

    lax.fori_loop(0, width // LANES, block, 0)
    pre = pre_ref[...]
    packed_ref[:, :width] = product((pre * jax.nn.sigmoid(pre)).astype(bf16), spread).astype(bf16)


def ema_backward_kernel(
    place_ref,
    x_ref, gain_ref, direct_ref, params_ref, spread_ref, table_ref, normed_ref, pre_ref,
    kept_ref, core_ref, near_ref, grad_shared_ref, grad_input_ref,
    down_kept_ref, down_core_ref, down_near_ref, blended_ref, offset_ref, *rest,
):
    weights = rest[:-8]
    (
        grad_row_ref, out_row_ref, vectors_ref, zero_ref, first_ref,
        smooth_ref, inner_ref, lag_ref,
    ) = rest[-8:]
    steps, width = x_ref.shape
    count = steps // SUBLANES
    sub = lax.broadcasted_iota(jnp.int32, (steps, LANES), 0)
    spread = spread_ref[...]

    down = down_kept_ref[:steps] + down_core_ref[:steps].astype(f32) + down_near_ref[...].astype(f32)
    down = right_inner(down.astype(bf16), spread)
    live = lax.broadcasted_iota(jnp.int32, (steps, 1), 0) < place_ref[2]
    out = blended_ref[...] + down + offset_ref[...]
    out_row_ref[...] = jnp.where(live, out, 0.0).astype(bf16)

    sums = kept_ref[:steps] + core_ref[:steps].astype(f32) + near_ref[...].astype(f32)
    span = weights[0].shape[1] - LANES
    smooth = sums[:, :width] + times_t(grad_shared_ref[...], weights, span, span + LANES)
    smooth_ref[...] = to_absolute(smooth, spread)
    inner_ref[...] = to_absolute(sums[:, width:], spread)

    def block(c, carry):
        columns = pl.ds(pl.multiple_of(c * LANES, LANES), LANES)
        pre = pre_ref[:, columns]
        grad_pre = smooth_ref[:, columns] * silu_slope(pre)
        normed = normed_ref[:, columns]
        vectors_ref[1:2, columns] = column_sum(grad_pre * normed)
        own = tiles_of(normed)
        total = tiles_of(inner_ref[:, columns] + direct_ref[:, columns] * grad_pre)
        for r in range(SUBLANES):
            moved = grad_pre
            if r:
                moved = jnp.where(sub < steps - r, pltpu.roll(grad_pre, steps - r, 0), 0.0)
            moved = tiles_of(moved)
            for q in range(count):
                w = row_tile(table_ref, q * SUBLANES + r, c)
                lag_sum = jnp.zeros((SUBLANES, LANES), f32)
                for i in range(count - q):
                    g = moved[i + q]
                    total[i] = total[i] + w * g
                    lag_sum = lag_sum + g * own[i]
                lag_ref[q * SUBLANES + r, pl.ds(c, 1), :] = column_sum(lag_sum)
        inner_ref[:, columns] = jnp.concatenate(total, axis=0)
        return carry

    lax.fori_loop(0, width // LANES, block, 0)

    keep_all = 1.0 - jax.nn.sigmoid(params_ref[0]) * jax.nn.sigmoid(params_ref[1])
    half = keep_all.shape[0] // 2
    for h in range(2):
        keep = keep_all[h * half : (h + 1) * half]

        def lag_step(lag, carry):
            power, zero, first = carry
            g = lag_ref[lag]
            first = first + (g * lag.astype(f32))[None] * power
            power = power * keep
            return (power, zero + g[None] * power, first)

        blank = jnp.zeros_like(keep)
        start = (jnp.ones_like(keep), blank + lag_ref[0][None], blank)
        unused, zero, first = lax.fori_loop(1, steps, lag_step, start)
        zero_ref[h * half : (h + 1) * half] = zero
        first_ref[h * half : (h + 1) * half] = first

    hat, scale = norm_parts(x_ref)
    grad = inner_ref[...]
    vectors_ref[0:1] = column_sum(grad * hat)
    grad = grad * gain_ref[...]
    grad = grad - jnp.mean(grad, axis=-1, keepdims=True) - hat * jnp.mean(
        grad * hat, axis=-1, keepdims=True
    )
    grad_row_ref[...] = (grad_input_ref[...] + scale * grad).astype(bf16)


def attention_kernel(
    place_ref, p0, p1, p2, p3, value_offset_ref, common_offset_ref, ask_gain_ref, ask_offset_ref,
    look_gain_ref, *rest,
):
    weights = rest[:-10]
    (
        value_pre_ref, value_ref, gates_kept_ref, gates_sent_ref, probs_low_ref, attended_ref,
        shared_pre_ref, query_ref, key_ref, probs_ref,
    ) = rest[-10:]
    steps = p0.shape[0]
    width = p0.shape[1] // 2
    span = value_ref.shape[1]
    gates_size = gates_kept_ref.shape[1]
    at = lax.broadcasted_iota(jnp.int32, (steps, steps), 0)
    to = lax.broadcasted_iota(jnp.int32, (steps, steps), 1)
    for p, packed in enumerate((p0, p1, p2, p3)):
        here = slice(p * steps, (p + 1) * steps)
        smooth = packed[:, :width]
        value_pre = times(packed[:, width:], weights, 0, span) + value_offset_ref[...]
        value_pre_ref[here] = value_pre
        value = (value_pre * sigma_of(value_pre)).astype(bf16)
        value_ref[here] = value
        gates = times(smooth, weights, span, span + gates_size)
        half = slice((p % 2) * steps, (p % 2 + 1) * steps)
        if p < 2:
            gates_kept_ref[half] = gates
        else:
            gates_sent_ref[half] = gates
        start = span + gates_size
        shared_pre = times(smooth, weights, start, start + LANES) + common_offset_ref[...]
        shared = shared_pre * sigma_of(shared_pre)
        query = (shared * ask_gain_ref[...] + ask_offset_ref[...]).astype(bf16)
        key = (shared * look_gain_ref[...]).astype(bf16)
        scores = right_inner(query, key) * (COMMON_SPAN_DIM ** (-0.5))
        allowed = (to <= at) & ((to < place_ref[2 + p]) | (to == at))
        scores = jnp.where(allowed, scores, -1e30)
        probs = jnp.exp(scores - jnp.max(scores, axis=-1, keepdims=True))
        probs = probs / jnp.sum(probs, axis=-1, keepdims=True)
        probs_low = probs.astype(bf16)
        probs_low_ref[here] = probs_low
        attended_ref[here] = product(probs_low, value)
        if p == 0:
            shared_pre_ref[...] = shared_pre
            query_ref[...] = query
            key_ref[...] = key
            probs_ref[...] = probs


def mix_kernel(p0, p1, p2, p3, offset_ref, attended_ref, *rest):
    weights = rest[:-4]
    reset_pre_ref, mixed_ref, kept_ref, sent_ref = rest[-4:]
    steps = p0.shape[0]
    width = p0.shape[1] // 2
    span = mixed_ref.shape[1]
    for p, packed in enumerate((p0, p1, p2, p3)):
        here = slice(p * steps, (p + 1) * steps)
        reset_pre = times(packed[:, :width], weights, 0, span) + offset_ref[...]
        reset_pre_ref[here] = reset_pre
        mixed = (reset_pre * sigma_of(reset_pre) * attended_ref[here]).astype(bf16)
        mixed_ref[here] = mixed
        part = times_t(mixed, weights, span, 2 * span)
        half = slice((p % 2) * steps, (p % 2 + 1) * steps)
        if p < 2:
            kept_ref[half] = part
        else:
            sent_ref[half] = part.astype(bf16)


def pick(index, own, other):
    zero = index == 0
    return [jnp.where(zero, own, other), jnp.where(zero, other, own)]


def hidden_kernel(
    place_ref, x_ref, kept_ref, core_ref, near_ref, gates_ref, gates_core_ref, gates_near_ref,
    update_offset_ref, hidden_offset_ref, gain_ref, spread_ref,
    hidden_pre_ref, update_ref, blended_ref, hat_ref, scale_ref, low_ref,
):
    steps = x_ref.shape[0]
    spread = spread_ref[...]
    part = kept_ref[:steps] + core_ref[:steps].astype(f32) + near_ref[...].astype(f32)
    size = gates_ref.shape[1] // 2
    sides = []
    for c, own in enumerate((gates_ref[:steps], gates_core_ref[:steps])):
        other = gates_near_ref[:, c * 2 * size : (c + 1) * 2 * size].astype(f32)
        sides.append(
            [
                jnp.concatenate(
                    pick(place_ref[0], own[:, k * size : (k + 1) * size], other[:, k * size : (k + 1) * size]),
                    axis=1,
                )
                for k in range(2)
            ]
        )
    whole = [jnp.concatenate(pick(place_ref[1], sides[0][k], sides[1][k]), axis=1) for k in range(2)]
    update = sigma_of(whole[0] + update_offset_ref[...])
    hidden_pre = whole[1] + hidden_offset_ref[...] + to_absolute(part, spread)
    hidden = hidden_pre * sigma_of(hidden_pre)
    values = x_ref[...].astype(f32)
    blended = values + update * (hidden - values)
    center = blended - jnp.mean(blended, axis=-1, keepdims=True)
    scale = lax.rsqrt(jnp.mean(center * center, axis=-1, keepdims=True) + epsilon)
    hat = center * scale
    hidden_pre_ref[...] = hidden_pre
    update_ref[...] = update
    blended_ref[...] = blended
    hat_ref[...] = hat
    scale_ref[...] = scale
    low_ref[...] = product((hat * gain_ref[...]).astype(bf16), spread).astype(bf16)


def ffn_kernel(first, count, *refs):
    f = refs[:4]
    seeds = refs[4:8]
    offset_ref = refs[8]
    at = 9
    if not first:
        down_before_ref, back_before_ref = refs[9:11]
        at = 11
    weights = refs[at : at + count]
    outs = refs[at + count :]
    grad_pre_ref, act_ref, bias_ref = outs[:3]
    steps = f[0].shape[0]
    width = f[0].shape[1]
    span = act_ref.shape[1]
    for p in range(4):
        here = slice(p * steps, (p + 1) * steps)
        pre = times(f[p][...], weights, 0, span) + offset_ref[...]
        sigma = sigma_of(pre)
        act = (pre * sigma).astype(bf16)
        act_ref[here] = act
        grad = times(seeds[p][...], weights, span, 2 * span)
        grad = (grad * (sigma * (1.0 + pre * (1.0 - sigma)))).astype(bf16)
        grad_pre_ref[here] = grad
        bias = column_sum(grad.astype(f32))
        bias_ref[...] = bias if p == 0 else bias_ref[...] + bias
        down = times_t(act, weights, span, 2 * span)
        back = times_t(grad, weights, 0, span)
        if first:
            down_ref, back_ref = outs[3:5]
            down_ref[here] = down
            back_ref[here] = back
            continue
        down = down + down_before_ref[here]
        back = back + back_before_ref[here]
        down_kept_ref, down_sent_ref, back_kept_ref, back_sent_ref = outs[3:7]
        half = slice((p % 2) * steps, (p % 2 + 1) * steps)
        if p < 2:
            down_kept_ref[half] = down
            back_kept_ref[half] = back
        else:
            down_sent_ref[half] = down.astype(bf16)
            back_sent_ref[half] = back.astype(bf16)


def blend_grad_kernel(
    place_ref, x_ref, seed_ref, kept_ref, core_ref, near_ref, hidden_pre_ref, update_ref, hat_ref,
    scale_ref, gain_ref, spread_ref,
    grad_input_ref, hidden_low_ref, update_low_ref, sums_ref,
):
    steps = x_ref.shape[0]
    spread = spread_ref[...]
    part = kept_ref[:steps] + core_ref[:steps].astype(f32) + near_ref[...].astype(f32)
    grad_norm = to_absolute(part, spread)
    hat = hat_ref[...]
    grad_hat = grad_norm * gain_ref[...]
    live = lax.broadcasted_iota(jnp.int32, (steps, 1), 0) < place_ref[2]
    seed = jnp.where(live, seed_ref[...].astype(f32), 0.0)
    grad_blended = seed + scale_ref[...] * (
        grad_hat
        - jnp.mean(grad_hat, axis=-1, keepdims=True)
        - hat * jnp.mean(grad_hat * hat, axis=-1, keepdims=True)
    )
    update = update_ref[...]
    hidden_pre = hidden_pre_ref[...]
    sigma = sigma_of(hidden_pre)
    values = x_ref[...].astype(f32)
    grad_input_ref[...] = grad_blended * (1.0 - update)
    grad_hidden = (
        grad_blended * update * (sigma * (1.0 + hidden_pre * (1.0 - sigma)))
    ).astype(bf16)
    grad_update = (
        grad_blended * (hidden_pre * sigma - values) * update * (1.0 - update)
    ).astype(bf16)
    hidden_low_ref[...] = product(grad_hidden, spread).astype(bf16)
    update_low_ref[...] = grad_update
    sums_ref[0:1] = column_sum(grad_update.astype(f32))
    sums_ref[1:2] = column_sum(grad_hidden.astype(f32))
    sums_ref[2:3] = column_sum(grad_norm * hat)


def attention_grad_kernel(
    h0, h1, h2, h3, reset_pre_ref, attended_ref, value_ref, value_pre_ref, probs_low_ref, *rest,
):
    weights = rest[:-5]
    grad_reset_ref, grad_value_ref, kept_ref, sent_ref, sums_ref = rest[-5:]
    steps = h0.shape[0]
    span = value_ref.shape[1]
    for p, h in enumerate((h0, h1, h2, h3)):
        here = slice(p * steps, (p + 1) * steps)
        grad_mixed = times(h[...], weights, span, 2 * span)
        reset_pre = reset_pre_ref[here]
        sigma = sigma_of(reset_pre)
        grad_attended = (grad_mixed * (reset_pre * sigma)).astype(bf16)
        grad_reset = (
            grad_mixed * attended_ref[here] * (sigma * (1.0 + reset_pre * (1.0 - sigma)))
        ).astype(bf16)
        grad_reset_ref[here] = grad_reset
        part = right_inner(grad_attended, value_ref[here])
        half = slice((p % 2) * steps, (p % 2 + 1) * steps)
        if p < 2:
            kept_ref[half] = part
        else:
            sent_ref[half] = part
        grad_value = left_inner(probs_low_ref[here], grad_attended)
        grad_value = (grad_value * silu_slope(value_pre_ref[here])).astype(bf16)
        grad_value_ref[here] = grad_value
        terms = (column_sum(grad_value.astype(f32)), column_sum(grad_reset.astype(f32)))
        for k, term in enumerate(terms):
            row = slice(k, k + 1)
            sums_ref[row] = term if p == 0 else sums_ref[row] + term


def input_grad_kernel(count, place_ref, *refs):
    h = refs[:4]
    u = refs[4:8]
    grad_reset_ref, grad_value_ref, spread_ref = refs[8:11]
    first = refs[11 : 11 + count]
    second = refs[11 + count : 11 + 2 * count]
    gates_ref, kept_ref, sent_ref = refs[11 + 2 * count :]
    steps, width = h[0].shape
    span = grad_value_ref.shape[1]
    size = gates_ref.shape[1] // 2
    gate = pl.ds(pl.multiple_of(place_ref[6], size), size)
    rows = spread_ref[gate, :]
    for p in range(4):
        here = slice(p * steps, (p + 1) * steps)
        gates = jnp.concatenate(
            [u[p][:, gate], right_inner(h[p][...], rows).astype(bf16)], axis=1
        )
        gates_ref[here] = gates
        smooth = times_t(grad_reset_ref[here], second, 0, span) + times_t(
            gates, first, span, span + 2 * size
        )
        norm = times_t(grad_value_ref[here], first, 0, span)
        half = slice((p % 2) * steps, (p % 2 + 1) * steps)
        if p < 2:
            kept_ref[half, :width] = smooth
            kept_ref[half, width:] = norm
        else:
            sent_ref[half, :width] = smooth.astype(bf16)
            sent_ref[half, width:] = norm.astype(bf16)


def score_grad_kernel(
    kept_ref, core_ref, near_ref, probs_ref, query_ref, key_ref, shared_pre_ref, ask_gain_ref,
    look_gain_ref, grad_shared_ref, sums_ref,
):
    steps = probs_ref.shape[0]
    grad_probs = kept_ref[:steps] + core_ref[:steps] + near_ref[...]
    probs = probs_ref[...]
    grad_scores = (
        probs * (grad_probs - jnp.sum(grad_probs * probs, axis=-1, keepdims=True))
    ).astype(bf16)
    scale = COMMON_SPAN_DIM ** (-0.5)
    grad_query = product(grad_scores, key_ref[...]) * scale
    grad_key = left_inner(grad_scores, query_ref[...]) * scale
    shared_pre = shared_pre_ref[...]
    sigma = sigma_of(shared_pre)
    shared = shared_pre * sigma
    grad_shared = (
        (grad_query * ask_gain_ref[...] + grad_key * look_gain_ref[...])
        * (sigma * (1.0 + shared_pre * (1.0 - sigma)))
    ).astype(bf16)
    grad_shared_ref[...] = grad_shared
    sums_ref[0:1] = column_sum(grad_shared.astype(f32))
    sums_ref[1:2] = column_sum(grad_query * shared)
    sums_ref[2:3] = column_sum(grad_query)
    sums_ref[3:4] = column_sum(grad_key * shared)


def weight_grad_kernel(plan, count, *refs):
    outs = refs[len(refs) - count :]
    at = 0
    for lefts, start, right in plan:
        columns = refs[right].shape[1]
        for k, out in enumerate(outs):
            size = out.shape[0]
            cut = slice(start + k * size, start + (k + 1) * size)
            left = jnp.concatenate([refs[i][:, cut] for i in lefts], axis=0)
            out[:, at : at + columns] = left_inner(left, refs[right][...]).astype(bf16)
        at += columns


def weight_grad(grid, name, width, plan, operands):
    count = grid.radix[0]
    columns = sum(operands[right].shape[1] for unused, start, right in plan)
    return call(
        functools.partial(weight_grad_kernel, plan, count),
        name,
        [((width // count, columns), bf16)] * count,
        operands,
    )


def per_device(
    grid,
    layer_entries,
    loss_sensitivity,
    occupied_counts,
    earlier_normalizer_gain,
    inflow_logits,
    decay_logits,
    channel_lifting,
    channel_collapse,
    direct_term_weight,
    content_projector,
    content_offset,
    common_projector,
    common_offset,
    asking_gain,
    asking_offset,
    lookup_gain,
    forget_gate_matrix,
    forget_gate_offset,
    renewal_gate_matrix,
    renewal_gate_offset,
    candidate_matrix,
    candidate_offset,
    attended_projector,
    later_normalizer_gain,
    hidden_layer_matrix,
    hidden_layer_offset,
    outward_layer_matrix,
    outward_layer_offset,
):
    core = lax.axis_index("mp")
    near = grid.near_index()
    micro, steps, width = layer_entries.shape
    half, quarter = width // 2, width // 4
    span = content_projector.shape[1] // 2
    ff = hidden_layer_matrix.shape[1] // 4
    swap_pairs = [(0, 1), (1, 0)]

    def swap(value):
        return lax.ppermute(value, "mp", swap_pairs)

    def group(own):
        near_own = grid.near_swap(own)
        return [own, near_own, swap(own), swap(near_own)]

    def gathered(kept, sent, near_type=bf16):
        came = swap(sent)
        rows = kept.shape[0] // 2
        near_part = (kept[rows:] + came[rows:].astype(f32)).astype(near_type)
        return kept, came, grid.near_swap(near_part)

    def ordered(index, own, other, axis):
        first = jnp.where(index == 0, own, other)
        second = jnp.where(index == 0, other, own)
        return jnp.concatenate([first, second], axis=axis)

    in_order = functools.partial(ordered, core)
    near_order = functools.partial(ordered, near)

    def cut(value, start, size, axis):
        return lax.dynamic_slice_in_dim(value, start, size, axis=axis)

    def chunks_of(side):
        gate = (2 * core + side) * quarter
        hidden = [side * 2 * ff, side * 2 * ff + ff]
        return [
            [
                cut(content_projector, side * span, span, 1),
                cut(renewal_gate_matrix, gate, quarter, 1),
                cut(candidate_matrix, gate, quarter, 1),
                common_projector,
            ],
            [
                cut(forget_gate_matrix, side * span, span, 1),
                cut(attended_projector, side * span, span, 0).T,
            ],
        ] + [
            [cut(hidden_layer_matrix, at, ff, 1), cut(outward_layer_matrix, at, ff, 0).T]
            for at in hidden
        ]

    gather = Gather(grid, chunks_of(near), chunks_of(1 - near))
    gather.advance()

    row_in = lax.dynamic_index_in_dim(layer_entries, core, 0, keepdims=False)
    row_seed = lax.dynamic_index_in_dim(loss_sensitivity, core, 0, keepdims=False)
    counts = ordered(core, occupied_counts[:1, 0], occupied_counts[1:, 0], 0)
    near_counts = grid.near_swap(counts)
    gate = (2 * core + near) * quarter
    place = jnp.stack(
        [near, core, counts[0], near_counts[0], counts[1], near_counts[1], gate]
    ).astype(jnp.int32)
    spread = grid.permutation(width)
    params = jnp.concatenate(
        [inflow_logits, decay_logits, channel_lifting, channel_collapse], axis=1
    )
    states = inflow_logits.shape[1]
    params = params.T.reshape(4, states, width // LANES, LANES)

    def line_of(value):
        return value.reshape(1, -1)

    gain, direct = line_of(earlier_normalizer_gain), line_of(direct_term_weight)
    tokens = 4 * steps
    normed, pre, packed, seed_low, table, seed_sum = call(
        ema_forward_kernel,
        "average_forward",
        [
            ((steps, width), f32),
            ((steps, width), f32),
            ((steps, 2 * width), bf16),
            ((steps, width), bf16),
            ((steps, width // LANES, LANES), f32),
            ((1, width), f32),
        ],
        [place, row_in, row_seed, gain, direct, params, spread],
        1,
    )
    gather.until(0) if gather.middle[1:] else None
    packed = gather.advance(packed)
    pieces = group(packed)
    seed_low = gather.advance(seed_low)
    near_seed = grid.near_swap(seed_low)
    w_first = gather.weights[0]
    blocks = len(w_first)

    value_pre, value, gates, gates_sent, probs_low, attended, shared_pre, query, key, probs = call(
        attention_kernel,
        "attention_forward",
        [
            ((tokens, span), f32),
            ((tokens, span), bf16),
            ((2 * steps, half), f32),
            ((2 * steps, half), f32),
            ((tokens, SPAN), bf16),
            ((tokens, span), f32),
            ((steps, LANES), f32),
            ((steps, LANES), bf16),
            ((steps, LANES), bf16),
            ((steps, SPAN), f32),
        ],
        [
            place,
            *pieces,
            line_of(cut(content_offset, near * span, span, 0)),
            line_of(common_offset),
            line_of(asking_gain),
            line_of(asking_offset),
            line_of(lookup_gain),
            *w_first,
        ],
        1,
    )
    gates_core = swap(gates_sent)
    attended, gates, gates_core, near_seed = gather.advance((attended, gates, gates_core, near_seed))
    seeds = [seed_low, near_seed, swap(seed_low), swap(near_seed)]
    gates_near = grid.near_swap(
        jnp.concatenate([gates[steps:], gates_core[steps:]], axis=1).astype(bf16)
    )
    w_second = gather.weights[1]
    reset_pre, mixed, mix_kept, mix_sent = call(
        mix_kernel,
        "reset_and_mix",
        [
            ((tokens, span), f32),
            ((tokens, span), bf16),
            ((2 * steps, width), f32),
            ((2 * steps, width), bf16),
        ],
        [*pieces, line_of(cut(forget_gate_offset, near * span, span, 0)), attended, *w_second],
    )
    mix_kept, mix_came = gather.advance((mix_kept, swap(mix_sent)))
    mix_near = grid.near_swap((mix_kept[steps:] + mix_came[steps:].astype(f32)).astype(bf16))
    hidden_pre, update, blended, hat, post_scale, ffn_low = call(
        hidden_kernel,
        "hidden_and_norm",
        [((steps, width), f32)] * 4 + [((steps, 1), f32), ((steps, width), bf16)],
        [
            place,
            row_in,
            mix_kept,
            mix_came,
            mix_near,
            gates,
            gates_core,
            gates_near,
            line_of(renewal_gate_offset),
            line_of(candidate_offset),
            line_of(later_normalizer_gain),
            spread,
        ],
        1,
    )
    ffn_pieces = group(ffn_low)
    while gather.stage < len(gather.state) + len(gather.middle):
        gather.advance()

    ffn_offset = line_of(cut(hidden_layer_offset, near * 2 * ff, 2 * ff, 0))
    moving = []
    bffnin = []
    before = []
    for at in range(2):
        first = at == 0
        out = [((tokens, ff), bf16), ((tokens, ff), bf16), ((1, ff), f32)]
        if first:
            out += [((tokens, width), f32)] * 2
        else:
            out += [((2 * steps, width), f32), ((2 * steps, width), bf16)] * 2
        grad_pre, act, bias, *before = call(
            functools.partial(ffn_kernel, first, blocks),
            "feed_forward",
            out,
            [*ffn_pieces, *seeds, ffn_offset[:, at * ff : (at + 1) * ff], *before, *gather.weights[2 + at]],
        )
        bffnin.append(bias[0])
        if not first:
            down_kept, down_sent, back_kept, back_sent = before
            came = swap(back_sent)
        parts = weight_grad(
            grid,
            "feed_forward_weights",
            width,
            (((0, 1, 2, 3), 0, 8), ((4, 5, 6, 7), 0, 9)),
            [*ffn_pieces, *seeds, grad_pre, act],
        )
        moving.append(Moving(grid, parts))
        if first:
            moving[0].across()
    near_part = (back_kept[steps:] + came[steps:].astype(f32)).astype(bf16)
    near_part = grid.near_swap(near_part)

    grad_input, grad_hidden, grad_update, row_sums = call(
        blend_grad_kernel,
        "blend_backward",
        [
            ((steps, width), f32),
            ((steps, width), bf16),
            ((steps, width), bf16),
            ((3, width), f32),
        ],
        [
            place,
            row_in,
            row_seed,
            back_kept,
            came,
            near_part,
            hidden_pre,
            update,
            hat,
            post_scale,
            line_of(later_normalizer_gain),
            spread,
        ],
        1,
    )
    (m_a, m_b) = moving
    m_a.value, m_b.parts, grad_hidden, grad_update = tie(
        (m_a.value, m_b.parts, grad_hidden, grad_update)
    )
    m_a.along()
    m_b.across()
    hidden_pieces = group(grad_hidden)
    update_pieces = group(grad_update)
    down = gathered(down_kept, down_sent)

    grad_reset, grad_value, probs_kept, probs_sent, span_sums = call(
        attention_grad_kernel,
        "attention_backward",
        [
            ((tokens, span), bf16),
            ((tokens, span), bf16),
            ((2 * steps, SPAN), f32),
            ((2 * steps, SPAN), f32),
            ((2, span), f32),
        ],
        [*hidden_pieces, reset_pre, attended, value, value_pre, probs_low, *w_second],
    )
    parts = weight_grad(
        grid,
        "reset_weights",
        width,
        (((0, 1, 2, 3), 0, 8), ((4, 5, 6, 7), 0, 9)),
        [*pieces, *hidden_pieces, grad_reset, mixed],
    )
    moving.append(Moving(grid, parts))
    m_c = moving[2]
    m_a.value, m_b.value, m_c.parts, grad_reset, grad_value = tie(
        (m_a.value, m_b.value, m_c.parts, grad_reset, grad_value)
    )
    m_b.along()
    m_c.across()
    probs_gathered = gathered(probs_kept, probs_sent, f32)
    grad_gates, in_kept, in_sent = call(
        functools.partial(input_grad_kernel, blocks),
        "input_backward",
        [((tokens, half), bf16), ((2 * steps, 2 * width), f32), ((2 * steps, 2 * width), bf16)],
        [place, *hidden_pieces, *update_pieces, grad_reset, grad_value, spread, *w_first, *w_second],
        1,
    )
    in_gathered = gathered(in_kept, in_sent)
    grad_shared, narrow = call(
        score_grad_kernel,
        "scores_backward",
        [((steps, LANES), bf16), ((4, LANES), f32)],
        [*probs_gathered, probs, query, key, shared_pre, line_of(asking_gain), line_of(lookup_gain)],
    )
    parts = weight_grad(
        grid,
        "value_weights",
        width,
        (((0, 1, 2, 3), width, 4), ((0, 1, 2, 3), 0, 5), ((0,), 0, 6)),
        [*pieces, grad_value, grad_gates, grad_shared],
    )
    moving.append(Moving(grid, parts))
    m_d = moving[3]
    m_b.value, m_c.value, m_d.parts = tie((m_b.value, m_c.value, m_d.parts))
    m_c.along()
    m_d.across()
    averages = call(
        ema_backward_kernel,
        "average_backward",
        [
            ((steps, width), bf16),
            ((steps, width), bf16),
            ((2, width), f32),
            (params.shape[1:], f32),
            (params.shape[1:], f32),
        ],
        [
            place,
            row_in,
            gain,
            direct,
            params,
            spread,
            table,
            normed,
            pre,
            *in_gathered,
            grad_shared,
            grad_input,
            *down,
            blended,
            line_of(outward_layer_offset),
            *w_first,
        ],
        1,
        [
            pltpu.VMEM((steps, width), f32),
            pltpu.VMEM((steps, width), f32),
            pltpu.VMEM((steps, width // LANES, LANES), f32),
        ],
    )
    m_c.value, m_d.value, averages = tie((m_c.value, m_d.value, averages))
    m_d.along()
    grad_row, out_row, grad_vectors, grad_zero, grad_first = averages

    lanes = COMMON_SPAN_DIM
    narrow = jnp.pad(narrow.reshape(1, -1), ((0, 0), (0, width - 4 * lanes)))
    shared_sums = jnp.concatenate(
        [
            grad_zero.reshape(states, width),
            grad_first.reshape(states, width),
            grad_vectors,
            row_sums,
            seed_sum,
            narrow,
            jnp.zeros((1, width), f32),
        ],
        axis=0,
    )
    kept = shared_sums.shape[0] // 2
    keep_rows = cut(shared_sums, core * kept, kept, 0) + swap(
        cut(shared_sums, (1 - core) * kept, kept, 0)
    )

    def placed(value):
        return near_order(value, jnp.zeros_like(value), 0).reshape(-1, width)

    wide_sums = [
        placed(span_sums[0]),
        placed(span_sums[1]),
        placed(jnp.concatenate(bffnin)),
    ]
    small = jnp.concatenate([keep_rows] + wide_sums, axis=0)
    sums = grid.sum_all(small)
    first_rows = sums[:kept]
    whole = in_order(first_rows, swap(first_rows), 0)
    wide = sums[kept:]
    zero = whole[:states].T
    first = whole[states : 2 * states].T
    rate = jax.nn.sigmoid(inflow_logits)
    damp = jax.nn.sigmoid(decay_logits)
    grad_collapse = rate * channel_lifting * zero
    grad_inflow = channel_collapse * zero
    grad_keep = channel_collapse * rate * channel_lifting * first
    grad_lifting = grad_inflow * rate
    grad_rate = (grad_inflow * channel_lifting - grad_keep * damp) * rate * (1.0 - rate)
    grad_damp = -grad_keep * rate * damp * (1.0 - damp)
    rest = whole[2 * states :]
    thin = rest[6].reshape(-1, lanes)

    (own_a, near_a), (own_b, near_b), (own_c, near_c), (own_d, near_d) = [m.near() for m in moving]
    out_in = near_order(
        jnp.concatenate([own_a[:, :ff], own_b[:, :ff]], axis=1),
        jnp.concatenate([near_a[:, :ff], near_b[:, :ff]], axis=1),
        1,
    )
    out_down = near_order(
        jnp.concatenate([own_a[:, ff:], own_b[:, ff:]], axis=1),
        jnp.concatenate([near_a[:, ff:], near_b[:, ff:]], axis=1),
        1,
    )
    out_reset = near_order(own_c[:, :span], near_c[:, :span], 1)
    out_wout = near_order(own_c[:, span:], near_c[:, span:], 1)
    out_value = near_order(own_d[:, :span], near_d[:, :span], 1)
    own_d, near_d = own_d[:, span:], near_d[:, span:]
    gates_half = jnp.concatenate(
        [
            near_order(own_d[:, :quarter], near_d[:, :quarter], 1),
            near_order(own_d[:, quarter:half], near_d[:, quarter:half], 1),
            own_d[:, half:] + near_d[:, half:],
        ],
        axis=1,
    )
    gates_other = swap(gates_half)
    out_update = in_order(gates_half[:, :half], gates_other[:, :half], 1)
    out_hidden = in_order(gates_half[:, half : 2 * half], gates_other[:, half : 2 * half], 1)
    out_shared = gates_half[:, 2 * half :] + gates_other[:, 2 * half :]

    rows_out = jnp.stack([out_row, grad_row])
    rows_other = swap(rows_out)
    outputs = in_order(rows_out[:1], rows_other[:1], 0)
    grad_tokens = in_order(rows_out[1:], rows_other[1:], 0)
    return (
        outputs,
        grad_tokens,
        rest[0],
        grad_rate,
        grad_damp,
        grad_lifting,
        grad_collapse,
        rest[1],
        out_value,
        wide[0],
        out_shared,
        thin[0],
        thin[1],
        thin[2],
        thin[3],
        out_reset,
        wide[1],
        out_update,
        rest[2],
        out_hidden,
        rest[3],
        out_wout.T,
        rest[4],
        out_in,
        wide[2:].reshape(-1),
        out_down.T,
        rest[5],
    )


def solution(mesh):
    grid = Grid(mesh.shape["dp"])
    return jax.shard_map(
        functools.partial(per_device, grid),
        mesh=mesh,
        in_specs=(
            P(None, "dp", None),
            P(None, "dp", None),
            P(None, "dp"),
            P(),
            P(),
            P(),
            P(),
            P(),
            P(),
            P("dp", "mp"),
            P("mp"),
            P("dp", None),
            P(),
            P(),
            P(),
            P(),
            P("dp", "mp"),
            P("mp"),
            P("dp", None),
            P(),
            P("dp", None),
            P(),
            P("mp", "dp"),
            P(),
            P("dp", "mp"),
            P("mp"),
            P("mp", "dp"),
            P(),
        ),
        out_specs=(
            P(None, "dp", None),
            P(None, "dp", None),
            P(),
            P(),
            P(),
            P(),
            P(),
            P(),
            P("dp", "mp"),
            P("mp"),
            P("dp", None),
            P(),
            P(),
            P(),
            P(),
            P("dp", "mp"),
            P("mp"),
            P("dp", None),
            P(),
            P("dp", None),
            P(),
            P("mp", "dp"),
            P(),
            P("dp", "mp"),
            P("mp"),
            P("mp", "dp"),
            P(),
        ),
        check_vma=False,
    )
```

```python
import functools

import jax
import jax.numpy as jnp
from jax import lax
from jax.experimental import pallas as pl
from jax.experimental.pallas import tpu as pltpu
from jax.sharding import PartitionSpec as P

COMMON_SPAN_DIM = 128
SPAN = 128
LANES = 128
SUBLANES = 8

epsilon = 1e-05
bf16 = jnp.bfloat16
f32 = jnp.float32


def product(left, right):
    return jnp.dot(left, right, preferred_element_type=f32)


def left_inner(left, right):
    return lax.dot_general(left, right, (((0,), (0,)), ((), ())), preferred_element_type=f32)


def right_inner(left, right):
    return lax.dot_general(left, right, (((1,), (1,)), ((), ())), preferred_element_type=f32)


def silu_slope(values):
    sigma = jax.nn.sigmoid(values)
    return sigma * (1.0 + values * (1.0 - sigma))


def radices_of(n):
    found = []
    left = n // 2
    while left > 1:
        r = 4 if left % 4 == 0 or not found and left > 4 else 2
        r = r if left % r == 0 else left
        found.append(r)
        left //= r
    while len(found) < 2:
        found.append(1)
    return tuple(found) + (2,)


class Grid:
    def __init__(self, n):
        self.n = n
        radix = radices_of(n)
        strides, left = [], n
        for r in radix:
            left //= r
            strides.append(left)
        self.radix = radix[1:-1] + radix[:1] + radix[-1:]
        self.stride = tuple(strides[1:-1] + strides[:1] + strides[-1:])
        self.near = len(radix) - 1
        self.line = len(radix) - 2

    def shift(self, dim, k):
        pairs = []
        for source in range(self.n):
            at = (source // self.stride[dim]) % self.radix[dim]
            to = (at + k) % self.radix[dim]
            pairs.append((source, source + (to - at) * self.stride[dim]))
        return pairs

    def fetch(self, array, dim):
        return [array] + [
            lax.ppermute(array, "dp", self.shift(dim, -k)) for k in range(1, self.radix[dim])
        ]

    def deliver(self, parts, dim):
        return [parts[0]] + [
            lax.ppermute(parts[k], "dp", self.shift(dim, k)) for k in range(1, self.radix[dim])
        ]

    def near_index(self):
        return lax.axis_index("dp") % 2

    def near_swap(self, value):
        return lax.ppermute(value, "dp", self.shift(self.near, 1))

    def sum_all(self, value):
        for dim in [self.near, *range(self.line), self.line]:
            r = self.radix[dim]
            got = self.fetch(value.astype(bf16) if dim == self.line else value, dim)
            got = [g.astype(f32) for g in got]
            if r == 4:
                value = (got[0] + got[2]) + (got[1] + got[3])
            elif r == 2:
                value = got[0] + got[1]
            elif r > 2:
                value = lax.psum(value, "dp", axis_index_groups=self.groups(dim))
        return value

    def groups(self, dim):
        lines = {}
        for i in range(self.n):
            at = (i // self.stride[dim]) % self.radix[dim]
            lines.setdefault(i - at * self.stride[dim], []).append(i)
        return list(lines.values())

    def permutation(self, width):
        rows = width // self.n
        me = lax.axis_index("dp")
        place = jnp.arange(width)
        block = place // rows
        absolute = place % rows + (block % 2) * rows
        block = block // 2
        for s, r in list(zip(self.stride, self.radix))[-2::-1]:
            absolute = absolute + ((block % r + (me // s) % r) % r) * (s * rows)
            block = block // r
        return (jnp.arange(width)[:, None] == absolute[None, :]).astype(bf16)


def total_of(parts):
    total = parts[0].astype(f32)
    for p in parts[1:]:
        total = total + p.astype(f32)
    return total


def tie(values):
    return lax.optimization_barrier(values)


class Gather:
    def __init__(self, grid, mine, theirs):
        self.grid = grid
        near = grid.near_index()
        pack = functools.partial(jnp.concatenate, axis=1)
        kept = [pack(chunk) for chunk in mine]
        sent = [pack(chunk) for chunk in theirs]

        def beside(own, other):
            return jnp.stack([jnp.where(near == 0, own, other), jnp.where(near == 0, other, own)])

        first = beside(kept[0], grid.near_swap(sent[0]))
        rest = pack(sent[1:])
        first, rest = tie((first, rest))
        rest = grid.near_swap(rest)
        self.state, at = [first], 0
        for own in kept[1:]:
            self.state.append(beside(own, rest[:, at : at + own.shape[1]]))
            at += own.shape[1]
        self.middle = list(range(grid.line - 1, -1, -1))
        self.weights = {}
        self.stage = 0

    def advance(self, held=None):
        stage, count = self.stage, len(self.state)
        active = [k for k in range(count) if 0 <= stage - k <= len(self.middle)]
        last = stage - 1 - len(self.middle)
        done = self.weights[last] if last in self.weights else []
        if stage:
            tied, done, held = tie(([self.state[k] for k in active], done, held))
            for k, value in zip(active, tied):
                self.state[k] = value
            if last in self.weights:
                self.weights[last] = done
        for k in active:
            step = stage - k
            dim = self.grid.line if step == 0 else self.middle[step - 1]
            got = self.grid.fetch(self.state[k], dim)
            if step < len(self.middle):
                self.state[k] = jnp.stack(got)
            else:
                self.weights[k] = [g.reshape(-1, g.shape[-1]) for g in got]
        self.stage += 1
        return held

    def until(self, k):
        while k not in self.weights:
            self.advance()


class Moving:
    def __init__(self, grid, parts):
        self.grid = grid
        shape = grid.radix[1:] + (-1, parts[0].shape[-1])
        self.parts = [p.reshape(shape) for p in parts]
        self.value = None

    def across(self):
        self.value = total_of(self.grid.deliver(self.parts, 0))
        for dim in range(1, self.grid.line):
            value = self.value.astype(bf16)
            self.value = total_of(
                self.grid.deliver([value[k] for k in range(self.grid.radix[dim])], dim)
            )
        self.value = self.value.astype(bf16)

    def along(self):
        parts = [self.value[k] for k in range(self.grid.radix[self.grid.line])]
        self.value = total_of(self.grid.deliver(parts, self.grid.line))

    def near(self, cuts=()):
        near = self.grid.near_index()
        kept = lax.dynamic_index_in_dim(self.value, near, 0, keepdims=False)
        sent = lax.dynamic_index_in_dim(self.value, 1 - near, 0, keepdims=False)
        edges = [0, *cuts, sent.shape[1]]
        came = [
            self.grid.near_swap(sent[:, a:b].astype(bf16)).astype(f32)
            for a, b in zip(edges, edges[1:])
        ]
        return (kept, *came)


def tiles_of(array):
    return [array[i * SUBLANES : (i + 1) * SUBLANES] for i in range(array.shape[0] // SUBLANES)]


def row_tile(table_ref, lag, c):
    row = table_ref[lag, pl.ds(c, 1), :]
    return jnp.broadcast_to(row, (SUBLANES, LANES))


def norm_parts(x_ref):
    values = x_ref[...].astype(f32)
    center = values - jnp.mean(values, axis=-1, keepdims=True)
    scale = lax.rsqrt(jnp.mean(center * center, axis=-1, keepdims=True) + epsilon)
    return center * scale, scale


def sigma_of(values):
    return jax.nn.sigmoid(values)


def call(kernel, name, out, operands, scalars=0, scratch=()):
    specs = [pl.BlockSpec(memory_space=pltpu.SMEM)] * scalars
    specs += [pl.BlockSpec(memory_space=pltpu.VMEM)] * (len(operands) - scalars)
    return pl.pallas_call(
        kernel,
        name=name,
        out_shape=[jax.ShapeDtypeStruct(shape, dtype) for shape, dtype in out],
        in_specs=specs,
        out_specs=[pl.BlockSpec(memory_space=pltpu.VMEM)] * len(out),
        scratch_shapes=list(scratch),
        cost_estimate=pl.CostEstimate(flops=1, bytes_accessed=1, transcendentals=0),
    )(*operands)


def times(x, blocks, start, stop):
    total, at = None, 0
    for w in blocks:
        rows = w.shape[0]
        term = product(x[:, at : at + rows], w[:, start:stop])
        total = term if total is None else total + term
        at += rows
    return total


def times_t(x, blocks, start, stop):
    return jnp.concatenate([right_inner(x, w[:, start:stop]) for w in blocks], axis=1)


def two_terms(value):
    high = value.astype(bf16)
    return [high, (value - high.astype(f32)).astype(bf16)]


def to_absolute(value, spread):
    rows = value.shape[0]
    out = right_inner(jnp.concatenate(two_terms(value), axis=0), spread)
    return out[:rows] + out[rows:]


def column_sum(values):
    return jnp.sum(values, axis=0, keepdims=True)


def ema_forward_kernel(
    place_ref, x_ref, seed_ref, gain_ref, direct_ref, params_ref, spread_ref,
    normed_ref, pre_ref, packed_ref, seed_low_ref, table_ref, seed_sum_ref,
):
    steps, width = x_ref.shape
    spread = spread_ref[...]
    hat, unused = norm_parts(x_ref)
    normed = hat * gain_ref[...]
    normed_ref[...] = normed
    live = lax.broadcasted_iota(jnp.int32, (steps, 1), 0) < place_ref[2]
    seed = jnp.where(live, seed_ref[...].astype(f32), 0.0)
    seed_sum_ref[...] = column_sum(seed)
    rate = jax.nn.sigmoid(params_ref[0])
    keep = 1.0 - rate * jax.nn.sigmoid(params_ref[1])
    weight = params_ref[3] * (rate * params_ref[2])

    def lag_step(lag, power):
        table_ref[lag] = jnp.sum(weight * power, axis=0)
        return power * keep

    lax.fori_loop(0, steps, lag_step, jnp.ones_like(keep))
    count = steps // SUBLANES
    sub = lax.broadcasted_iota(jnp.int32, (steps, LANES), 0)

    def block(c, carry):
        columns = pl.ds(pl.multiple_of(c * LANES, LANES), LANES)
        base = normed_ref[:, columns]
        total = [jnp.zeros((SUBLANES, LANES), f32)] * count
        for r in range(SUBLANES):
            moved = base if r == 0 else jnp.where(sub >= r, pltpu.roll(base, r, 0), 0.0)
            moved = tiles_of(moved)
            for q in range(count):
                w = row_tile(table_ref, q * SUBLANES + r, c)
                for i in range(q, count):
                    total[i] = total[i] + w * moved[i - q]
        pre_ref[:, columns] = jnp.concatenate(total, axis=0) + direct_ref[:, columns] * base
        return carry

    lax.fori_loop(0, width // LANES, block, 0)
    pre = pre_ref[...]
    smooth = (pre * jax.nn.sigmoid(pre)).astype(bf16)
    rows = jnp.concatenate([smooth, normed_ref[...].astype(bf16), seed.astype(bf16)], axis=0)
    rows = product(rows, spread).astype(bf16)
    packed_ref[:, :width] = rows[:steps]
    packed_ref[:, width:] = rows[steps : 2 * steps]
    seed_low_ref[...] = rows[2 * steps :]


def ema_backward_kernel(
    place_ref,
    x_ref, gain_ref, direct_ref, params_ref, spread_ref, table_ref, normed_ref, pre_ref,
    kept_ref, core_0, core_1, core_2, core_3, near_ref,
    grad_shared_ref, grad_input_ref, row_sums_ref, seed_sum_ref,
    narrow_ref, down_kept_ref, down_core_ref, down_near_ref, blended_ref, offset_ref, *rest,
):
    weights = rest[:-7]
    grad_row_ref, out_row_ref, keep_ref, send_ref, smooth_ref, inner_ref, lag_ref = rest[-7:]
    vectors_ref = send_ref
    steps, width = x_ref.shape
    count = steps // SUBLANES
    sub = lax.broadcasted_iota(jnp.int32, (steps, LANES), 0)
    spread = spread_ref[...]

    down = down_kept_ref[:steps] + down_core_ref[:steps].astype(f32) + down_near_ref[...].astype(f32)
    core = [p[:steps].astype(f32) for p in (core_0, core_1, core_2, core_3)]
    sums = kept_ref[:steps] + jnp.concatenate(core, axis=1) + near_ref[...].astype(f32)
    smooth, norm = sums[:, :width], sums[:, width:]
    span = weights[0].shape[1] - LANES
    smooth = smooth + times_t(grad_shared_ref[...], weights, span, span + LANES)
    terms = [down.astype(bf16), *two_terms(smooth), *two_terms(norm)]
    out = right_inner(jnp.concatenate(terms, axis=0), spread)
    smooth_ref[...] = out[steps : 2 * steps] + out[2 * steps : 3 * steps]
    inner_ref[...] = out[3 * steps : 4 * steps] + out[4 * steps :]
    live = lax.broadcasted_iota(jnp.int32, (steps, 1), 0) < place_ref[2]
    out_row = blended_ref[...] + out[:steps] + offset_ref[...]
    out_row_ref[...] = jnp.where(live, out_row, 0.0).astype(bf16)

    def block(c, carry):
        columns = pl.ds(pl.multiple_of(c * LANES, LANES), LANES)
        pre = pre_ref[:, columns]
        grad_pre = smooth_ref[:, columns] * silu_slope(pre)
        normed = normed_ref[:, columns]
        vectors_ref[1:2, columns] = column_sum(grad_pre * normed)
        own = tiles_of(normed)
        total = tiles_of(inner_ref[:, columns] + direct_ref[:, columns] * grad_pre)
        for r in range(SUBLANES):
            moved = grad_pre
            if r:
                moved = jnp.where(sub < steps - r, pltpu.roll(grad_pre, steps - r, 0), 0.0)
            moved = tiles_of(moved)
            for q in range(count):
                w = row_tile(table_ref, q * SUBLANES + r, c)
                lag_sum = jnp.zeros((SUBLANES, LANES), f32)
                for i in range(count - q):
                    g = moved[i + q]
                    total[i] = total[i] + w * g
                    lag_sum = lag_sum + g * own[i]
                lag_ref[q * SUBLANES + r, pl.ds(c, 1), :] = column_sum(lag_sum)
        inner_ref[:, columns] = jnp.concatenate(total, axis=0)
        return carry

    lax.fori_loop(0, width // LANES, block, 0)

    keep_all = 1.0 - jax.nn.sigmoid(params_ref[0]) * jax.nn.sigmoid(params_ref[1])
    states = keep_all.shape[0]
    half = states // 2
    sums_of_lags = [[], []]
    for h in range(2):
        keep = keep_all[h * half : (h + 1) * half]

        def lag_step(lag, carry):
            power, zero, first = carry
            g = lag_ref[lag]
            first = first + (g * lag.astype(f32))[None] * power
            power = power * keep
            return (power, zero + g[None] * power, first)

        blank = jnp.zeros_like(keep)
        start = (jnp.ones_like(keep), blank + lag_ref[0][None], blank)
        unused, zero, first = lax.fori_loop(1, steps, lag_step, start)
        sums_of_lags[0].append(zero)
        sums_of_lags[1].append(first)

    hat, scale = norm_parts(x_ref)
    grad = inner_ref[...]
    prenorm = column_sum(grad * hat)
    grad = grad * gain_ref[...]
    grad = grad - jnp.mean(grad, axis=-1, keepdims=True) - hat * jnp.mean(
        grad * hat, axis=-1, keepdims=True
    )
    grad_row_ref[...] = (grad_input_ref[...] + scale * grad).astype(bf16)

    def flat(states_first):
        blocks = range(width // LANES)
        return jnp.concatenate([states_first[:, c] for c in blocks], axis=1)

    zero, first = [flat(jnp.concatenate(part, axis=0)) for part in sums_of_lags]
    narrow = jnp.concatenate([narrow_ref[k : k + 1] for k in range(4)], axis=1)
    narrow = jnp.concatenate([narrow, jnp.zeros((1, width - narrow.shape[1]), f32)], axis=1)
    rest_rows = [prenorm, vectors_ref[1:2], row_sums_ref[...], seed_sum_ref[...], narrow]
    rest_rows = jnp.concatenate(rest_rows + [jnp.zeros((1, width), f32)], axis=0)
    keep, send = pick(place_ref[1], zero, first)
    keep_rest, send_rest = pick(place_ref[1], rest_rows, jnp.zeros_like(rest_rows))
    keep_ref[:states] = keep
    keep_ref[states:] = keep_rest
    send_ref[:states] = send
    send_ref[states:] = send_rest


def attention_kernel(
    place_ref, p0, p1, p2, p3, value_offset_ref, common_offset_ref, ask_gain_ref, ask_offset_ref,
    look_gain_ref, *rest,
):
    weights = rest[:-11]
    (
        value_pre_ref, value_ref, gates_ref, gates_core_ref, gates_near_ref, probs_low_ref,
        attended_ref, shared_pre_ref, query_ref, key_ref, probs_ref,
    ) = rest[-11:]
    steps = p0.shape[0]
    width = p0.shape[1] // 2
    span = value_ref.shape[1]
    gates_size = gates_ref.shape[1]
    at = lax.broadcasted_iota(jnp.int32, (steps, steps), 0)
    to = lax.broadcasted_iota(jnp.int32, (steps, steps), 1)
    pieces = (p0, p1, p2, p3)
    smooth = jnp.concatenate([p[:, :width] for p in pieces], axis=0)
    norm = jnp.concatenate([p[:, width:] for p in pieces], axis=0)
    value_pre = times(norm, weights, 0, span) + value_offset_ref[...]
    value_pre_ref[...] = value_pre
    value_ref[...] = (value_pre * sigma_of(value_pre)).astype(bf16)
    gates = times(smooth, weights, span, span + gates_size)
    gates_ref[...] = gates[:steps]
    gates_core_ref[...] = gates[2 * steps : 3 * steps]
    gates_near_ref[:steps] = gates[steps : 2 * steps].astype(bf16)
    gates_near_ref[steps:] = gates[3 * steps :].astype(bf16)
    start = span + gates_size
    shared_pre = times(smooth, weights, start, start + LANES) + common_offset_ref[...]
    shared = shared_pre * sigma_of(shared_pre)
    query = (shared * ask_gain_ref[...] + ask_offset_ref[...]).astype(bf16)
    key = (shared * look_gain_ref[...]).astype(bf16)
    shared_pre_ref[...] = shared_pre[:steps]
    query_ref[...] = query[:steps]
    key_ref[...] = key[:steps]
    for p in range(4):
        here = slice(p * steps, (p + 1) * steps)
        scores = right_inner(query[here], key[here]) * (COMMON_SPAN_DIM ** (-0.5))
        allowed = (to <= at) & ((to < place_ref[2 + p]) | (to == at))
        scores = jnp.where(allowed, scores, -1e30)
        probs = jnp.exp(scores - jnp.max(scores, axis=-1, keepdims=True))
        probs = probs / jnp.sum(probs, axis=-1, keepdims=True)
        probs_low = probs.astype(bf16)
        probs_low_ref[here] = probs_low
        attended_ref[here] = product(probs_low, value_ref[here])
        if p == 0:
            probs_ref[...] = probs


def mix_kernel(p0, p1, p2, p3, offset_ref, attended_ref, *rest):
    weights = rest[:-4]
    reset_pre_ref, mixed_ref, kept_ref, sent_ref = rest[-4:]
    steps = p0.shape[0]
    width = p0.shape[1] // 2
    span = mixed_ref.shape[1]
    smooth = jnp.concatenate([p[:, :width] for p in (p0, p1, p2, p3)], axis=0)
    reset_pre = times(smooth, weights, 0, span) + offset_ref[...]
    reset_pre_ref[...] = reset_pre
    mixed = (reset_pre * sigma_of(reset_pre) * attended_ref[...]).astype(bf16)
    mixed_ref[...] = mixed
    part = times_t(mixed, weights, span, 2 * span)
    kept_ref[...] = part[: 2 * steps]
    sent_ref[...] = part[2 * steps :].astype(bf16)


def pick(index, own, other):
    zero = index == 0
    return [jnp.where(zero, own, other), jnp.where(zero, other, own)]


def hidden_kernel(
    place_ref, x_ref, kept_ref, core_ref, near_ref,
    gates_ref, gates_core_ref, gates_near_ref, gates_far_ref,
    update_offset_ref, hidden_offset_ref, gain_ref, spread_ref,
    hidden_pre_ref, update_ref, blended_ref, hat_ref, scale_ref, low_ref,
):
    steps = x_ref.shape[0]
    spread = spread_ref[...]
    part = kept_ref[:steps] + core_ref[:steps].astype(f32) + near_ref[...].astype(f32)
    size = gates_ref.shape[1] // 2
    sides = []
    for own, other in (
        (gates_ref[...], gates_near_ref[:steps].astype(f32)),
        (gates_core_ref[...], gates_far_ref[...].astype(f32)),
    ):
        sides.append(
            [
                jnp.concatenate(
                    pick(place_ref[0], own[:, k * size : (k + 1) * size], other[:, k * size : (k + 1) * size]),
                    axis=1,
                )
                for k in range(2)
            ]
        )
    whole = [jnp.concatenate(pick(place_ref[1], sides[0][k], sides[1][k]), axis=1) for k in range(2)]
    update = sigma_of(whole[0] + update_offset_ref[...])
    hidden_pre = whole[1] + hidden_offset_ref[...] + to_absolute(part, spread)
    hidden = hidden_pre * sigma_of(hidden_pre)
    values = x_ref[...].astype(f32)
    blended = values + update * (hidden - values)
    center = blended - jnp.mean(blended, axis=-1, keepdims=True)
    scale = lax.rsqrt(jnp.mean(center * center, axis=-1, keepdims=True) + epsilon)
    hat = center * scale
    hidden_pre_ref[...] = hidden_pre
    update_ref[...] = update
    blended_ref[...] = blended
    hat_ref[...] = hat
    scale_ref[...] = scale
    low_ref[...] = product((hat * gain_ref[...]).astype(bf16), spread).astype(bf16)


def ffn_kernel(first, count, *refs):
    f = refs[:4]
    seeds = refs[4:8]
    offset_ref = refs[8]
    at = 9
    if not first:
        down_before_ref, back_before_ref = refs[9:11]
        at = 11
    weights = refs[at : at + count]
    outs = refs[at + count :]
    grad_pre_ref, act_ref, bias_ref = outs[:3]
    steps = f[0].shape[0]
    span = act_ref.shape[1]
    pre = times(jnp.concatenate([p[...] for p in f], axis=0), weights, 0, span) + offset_ref[...]
    sigma = sigma_of(pre)
    act = (pre * sigma).astype(bf16)
    act_ref[...] = act
    seed = jnp.concatenate([p[...] for p in seeds], axis=0)
    grad = times(seed, weights, span, 2 * span)
    grad = (grad * (sigma * (1.0 + pre * (1.0 - sigma)))).astype(bf16)
    grad_pre_ref[...] = grad
    bias_ref[...] = column_sum(grad.astype(f32))
    down = times_t(act, weights, span, 2 * span)
    back = times_t(grad, weights, 0, span)
    if first:
        down_ref, back_ref = outs[3:5]
        down_ref[...] = down
        back_ref[...] = back
        return
    down_kept_ref, down_sent_ref, back_kept_ref, back_sent_ref = outs[3:7]
    down = down + down_before_ref[...]
    down_kept_ref[...] = down[: 2 * steps]
    down_sent_ref[...] = down[2 * steps :].astype(bf16)
    back = back + back_before_ref[...]
    back_kept_ref[...] = back[: 2 * steps]
    back_sent_ref[...] = back[2 * steps :].astype(bf16)


def blend_grad_kernel(
    place_ref, x_ref, seed_ref, kept_ref, core_ref, near_ref, hidden_pre_ref, update_ref, hat_ref,
    scale_ref, gain_ref, spread_ref,
    grad_input_ref, packed_ref, sums_ref,
):
    steps, width = x_ref.shape
    spread = spread_ref[...]
    part = kept_ref[:steps] + core_ref[:steps].astype(f32) + near_ref[...].astype(f32)
    grad_norm = to_absolute(part, spread)
    hat = hat_ref[...]
    grad_hat = grad_norm * gain_ref[...]
    live = lax.broadcasted_iota(jnp.int32, (steps, 1), 0) < place_ref[2]
    seed = jnp.where(live, seed_ref[...].astype(f32), 0.0)
    grad_blended = seed + scale_ref[...] * (
        grad_hat
        - jnp.mean(grad_hat, axis=-1, keepdims=True)
        - hat * jnp.mean(grad_hat * hat, axis=-1, keepdims=True)
    )
    update = update_ref[...]
    hidden_pre = hidden_pre_ref[...]
    sigma = sigma_of(hidden_pre)
    values = x_ref[...].astype(f32)
    grad_input_ref[...] = grad_blended * (1.0 - update)
    grad_hidden = (
        grad_blended * update * (sigma * (1.0 + hidden_pre * (1.0 - sigma)))
    ).astype(bf16)
    grad_update = (
        grad_blended * (hidden_pre * sigma - values) * update * (1.0 - update)
    ).astype(bf16)
    packed_ref[:, :width] = product(grad_hidden, spread).astype(bf16)
    packed_ref[:, width:] = grad_update
    sums_ref[0:1] = column_sum(grad_update.astype(f32))
    sums_ref[1:2] = column_sum(grad_hidden.astype(f32))
    sums_ref[2:3] = column_sum(grad_norm * hat)


def attention_grad_kernel(
    h0, h1, h2, h3, reset_pre_ref, attended_ref, value_ref, value_pre_ref, probs_low_ref, *rest,
):
    weights = rest[:-5]
    grad_reset_ref, grad_value_ref, kept_ref, sent_ref, sums_ref = rest[-5:]
    steps = h0.shape[0]
    span = value_ref.shape[1]
    grad_mixed = times(
        jnp.concatenate([h[:, : h.shape[1] // 2] for h in (h0, h1, h2, h3)], axis=0),
        weights,
        span,
        2 * span,
    )
    reset_pre = reset_pre_ref[...]
    sigma = sigma_of(reset_pre)
    grad_attended = (grad_mixed * (reset_pre * sigma)).astype(bf16)
    grad_reset = (
        grad_mixed * attended_ref[...] * (sigma * (1.0 + reset_pre * (1.0 - sigma)))
    ).astype(bf16)
    grad_reset_ref[...] = grad_reset
    sums_ref[1:2] = column_sum(grad_reset.astype(f32))
    for p in range(4):
        here = slice(p * steps, (p + 1) * steps)
        part = right_inner(grad_attended[here], value_ref[here])
        half = slice((p % 2) * steps, (p % 2 + 1) * steps)
        if p < 2:
            kept_ref[half] = part
        else:
            sent_ref[half] = part
        grad_value = left_inner(probs_low_ref[here], grad_attended[here])
        grad_value = (grad_value * silu_slope(value_pre_ref[here])).astype(bf16)
        grad_value_ref[here] = grad_value
        term = column_sum(grad_value.astype(f32))
        sums_ref[0:1] = term if p == 0 else sums_ref[0:1] + term


def input_grad_kernel(count, place_ref, *refs):
    h = refs[:4]
    grad_reset_ref, grad_value_ref, spread_ref = refs[4:7]
    first = refs[7 : 7 + count]
    second = refs[7 + count : 7 + 2 * count]
    gates_ref, kept_ref, *sent = refs[7 + 2 * count :]
    steps = h[0].shape[0]
    width = h[0].shape[1] // 2
    span = grad_value_ref.shape[1]
    size = gates_ref.shape[1] // 2
    gate = pl.ds(pl.multiple_of(place_ref[6], size), size)
    rows = spread_ref[gate, :]
    late = pl.ds(pl.multiple_of(width + place_ref[6], size), size)
    update = jnp.concatenate([p[:, late] for p in h], axis=0)
    hidden = right_inner(jnp.concatenate([p[:, :width] for p in h], axis=0), rows).astype(bf16)
    gates = jnp.concatenate([update, hidden], axis=1)
    gates_ref[...] = gates
    smooth = times_t(grad_reset_ref[...], second, 0, span) + times_t(
        gates, first, span, span + 2 * size
    )
    norm = times_t(grad_value_ref[...], first, 0, span)
    kept_ref[:, :width] = smooth[: 2 * steps]
    kept_ref[:, width:] = norm[: 2 * steps]
    for k, out in enumerate(sent):
        part = (smooth, norm)[k // 2][2 * steps :]
        at = (k % 2) * out.shape[1]
        out[...] = part[:, at : at + out.shape[1]].astype(bf16)


def score_grad_kernel(
    kept_ref, core_ref, near_ref, probs_ref, query_ref, key_ref, shared_pre_ref, ask_gain_ref,
    look_gain_ref, grad_shared_ref, sums_ref,
):
    steps = probs_ref.shape[0]
    grad_probs = kept_ref[:steps] + core_ref[:steps] + near_ref[...]
    probs = probs_ref[...]
    grad_scores = (
        probs * (grad_probs - jnp.sum(grad_probs * probs, axis=-1, keepdims=True))
    ).astype(bf16)
    scale = COMMON_SPAN_DIM ** (-0.5)
    grad_query = product(grad_scores, key_ref[...]) * scale
    grad_key = left_inner(grad_scores, query_ref[...]) * scale
    shared_pre = shared_pre_ref[...]
    sigma = sigma_of(shared_pre)
    shared = shared_pre * sigma
    grad_shared = (
        (grad_query * ask_gain_ref[...] + grad_key * look_gain_ref[...])
        * (sigma * (1.0 + shared_pre * (1.0 - sigma)))
    ).astype(bf16)
    grad_shared_ref[...] = grad_shared
    sums_ref[0:1] = column_sum(grad_shared.astype(f32))
    sums_ref[1:2] = column_sum(grad_query * shared)
    sums_ref[2:3] = column_sum(grad_query)
    sums_ref[3:4] = column_sum(grad_key * shared)


def weight_grad_kernel(plan, count, *refs):
    outs = refs[len(refs) - count :]
    at = 0
    for lefts, start, right in plan:
        columns = refs[right].shape[1]
        for k, out in enumerate(outs):
            size = out.shape[0]
            cut = slice(start + k * size, start + (k + 1) * size)
            left = jnp.concatenate([refs[i][:, cut] for i in lefts], axis=0)
            out[:, at : at + columns] = left_inner(left, refs[right][...]).astype(bf16)
        at += columns


def weight_grad(grid, name, width, plan, operands):
    count = grid.radix[0]
    columns = sum(operands[right].shape[1] for unused, start, right in plan)
    return call(
        functools.partial(weight_grad_kernel, plan, count),
        name,
        [((width // count, columns), bf16)] * count,
        operands,
    )


def per_device(
    grid,
    layer_entries,
    loss_sensitivity,
    occupied_counts,
    earlier_normalizer_gain,
    inflow_logits,
    decay_logits,
    channel_lifting,
    channel_collapse,
    direct_term_weight,
    content_projector,
    content_offset,
    common_projector,
    common_offset,
    asking_gain,
    asking_offset,
    lookup_gain,
    forget_gate_matrix,
    forget_gate_offset,
    renewal_gate_matrix,
    renewal_gate_offset,
    candidate_matrix,
    candidate_offset,
    attended_projector,
    later_normalizer_gain,
    hidden_layer_matrix,
    hidden_layer_offset,
    outward_layer_matrix,
    outward_layer_offset,
):
    core = lax.axis_index("mp")
    near = grid.near_index()
    micro, steps, width = layer_entries.shape
    half, quarter = width // 2, width // 4
    span = content_projector.shape[1] // 2
    ff = hidden_layer_matrix.shape[1] // 4
    swap_pairs = [(0, 1), (1, 0)]

    def swap(value):
        return lax.ppermute(value, "mp", swap_pairs)

    def group(own):
        near_own = grid.near_swap(own)
        return [own, near_own, swap(own), swap(near_own)]

    def gathered(kept, sent, near_type=bf16):
        came = swap(sent)
        rows = kept.shape[0] // 2
        near_part = (kept[rows:] + came[rows:].astype(f32)).astype(near_type)
        return kept, came, grid.near_swap(near_part)

    def ordered(index, own, other, axis):
        first = jnp.where(index == 0, own, other)
        second = jnp.where(index == 0, other, own)
        return jnp.concatenate([first, second], axis=axis)

    in_order = functools.partial(ordered, core)
    near_order = functools.partial(ordered, near)

    def cut(value, start, size, axis):
        return lax.dynamic_slice_in_dim(value, start, size, axis=axis)

    def chunks_of(side):
        gate = (2 * core + side) * quarter
        hidden = [side * 2 * ff, side * 2 * ff + ff]
        return [
            [
                cut(content_projector, side * span, span, 1),
                cut(renewal_gate_matrix, gate, quarter, 1),
                cut(candidate_matrix, gate, quarter, 1),
                common_projector,
            ],
            [
                cut(forget_gate_matrix, side * span, span, 1),
                cut(attended_projector, side * span, span, 0).T,
            ],
        ] + [
            [cut(hidden_layer_matrix, at, ff, 1), cut(outward_layer_matrix, at, ff, 0).T]
            for at in hidden
        ]

    gather = Gather(grid, chunks_of(near), chunks_of(1 - near))
    gather.advance()

    row_in = lax.dynamic_index_in_dim(layer_entries, core, 0, keepdims=False)
    row_seed = lax.dynamic_index_in_dim(loss_sensitivity, core, 0, keepdims=False)
    counts = ordered(core, occupied_counts[:1, 0], occupied_counts[1:, 0], 0)
    near_counts = grid.near_swap(counts)
    gate = (2 * core + near) * quarter
    place = jnp.stack(
        [near, core, counts[0], near_counts[0], counts[1], near_counts[1], gate]
    ).astype(jnp.int32)
    spread = grid.permutation(width)
    params = jnp.concatenate(
        [inflow_logits, decay_logits, channel_lifting, channel_collapse], axis=1
    )
    states = inflow_logits.shape[1]
    params = params.T.reshape(4, states, width // LANES, LANES)

    def line_of(value):
        return value.reshape(1, -1)

    gain, direct = line_of(earlier_normalizer_gain), line_of(direct_term_weight)
    tokens = 4 * steps
    normed, pre, packed, seed_low, table, seed_sum = call(
        ema_forward_kernel,
        "average_forward",
        [
            ((steps, width), f32),
            ((steps, width), f32),
            ((steps, 2 * width), bf16),
            ((steps, width), bf16),
            ((steps, width // LANES, LANES), f32),
            ((1, width), f32),
        ],
        [place, row_in, row_seed, gain, direct, params, spread],
        1,
    )
    gather.until(0) if gather.middle[1:] else None
    packed = gather.advance(packed)
    pieces = group(packed)
    seed_low = gather.advance(seed_low)
    near_seed = grid.near_swap(seed_low)
    w_first = gather.weights[0]
    blocks = len(w_first)

    (
        value_pre, value, gates, gates_core, gates_near, probs_low, attended, shared_pre, query, key, probs
    ) = call(
        attention_kernel,
        "attention_forward",
        [
            ((tokens, span), f32),
            ((tokens, span), bf16),
            ((steps, half), f32),
            ((steps, half), f32),
            ((2 * steps, half), bf16),
            ((tokens, SPAN), bf16),
            ((tokens, span), f32),
            ((steps, LANES), f32),
            ((steps, LANES), bf16),
            ((steps, LANES), bf16),
            ((steps, SPAN), f32),
        ],
        [
            place,
            *pieces,
            line_of(cut(content_offset, near * span, span, 0)),
            line_of(common_offset),
            line_of(asking_gain),
            line_of(asking_offset),
            line_of(lookup_gain),
            *w_first,
        ],
        1,
    )
    attended, gates_near, gates_core, near_seed = gather.advance(
        (attended, gates_near, gates_core, near_seed)
    )
    seeds = [seed_low, near_seed, swap(seed_low), swap(near_seed)]
    gates_near = grid.near_swap(gates_near)
    w_second = gather.weights[1]
    reset_pre, mixed, mix_kept, mix_sent = call(
        mix_kernel,
        "reset_and_mix",
        [
            ((tokens, span), f32),
            ((tokens, span), bf16),
            ((2 * steps, width), f32),
            ((2 * steps, width), bf16),
        ],
        [*pieces, line_of(cut(forget_gate_offset, near * span, span, 0)), attended, *w_second],
    )
    mix_kept, mix_sent, gates_near = gather.advance((mix_kept, mix_sent, gates_near))
    mix_came = swap(mix_sent)
    mix_near = grid.near_swap((mix_kept[steps:] + mix_came[steps:].astype(f32)).astype(bf16))
    hidden_pre, update, blended, hat, post_scale, ffn_low = call(
        hidden_kernel,
        "hidden_and_norm",
        [((steps, width), f32)] * 4 + [((steps, 1), f32), ((steps, width), bf16)],
        [
            place,
            row_in,
            mix_kept,
            mix_came,
            mix_near,
            gates,
            swap(gates_core),
            gates_near,
            swap(gates_near[steps:]),
            line_of(renewal_gate_offset),
            line_of(candidate_offset),
            line_of(later_normalizer_gain),
            spread,
        ],
        1,
    )
    ffn_pieces = group(ffn_low)
    while gather.stage < len(gather.state) + len(gather.middle):
        gather.advance()

    ffn_offset = line_of(cut(hidden_layer_offset, near * 2 * ff, 2 * ff, 0))
    moving = []
    bffnin = []
    before = []
    for at in range(2):
        first = at == 0
        out = [((tokens, ff), bf16), ((tokens, ff), bf16), ((1, ff), f32)]
        if first:
            out += [((tokens, width), f32)] * 2
        else:
            out += [((2 * steps, width), f32), ((2 * steps, width), bf16)] * 2
        grad_pre, act, bias, *before = call(
            functools.partial(ffn_kernel, first, blocks),
            "feed_forward",
            out,
            [*ffn_pieces, *seeds, ffn_offset[:, at * ff : (at + 1) * ff], *before, *gather.weights[2 + at]],
        )
        bffnin.append(bias[0])
        if not first:
            down_kept, down_sent, back_kept, back_sent = before
            came = swap(back_sent)
        parts = weight_grad(
            grid,
            "feed_forward_weights",
            width,
            (((0, 1, 2, 3), 0, 8), ((4, 5, 6, 7), 0, 9)),
            [*ffn_pieces, *seeds, grad_pre, act],
        )
        moving.append(Moving(grid, parts))
        if first:
            moving[0].across()
    near_part = (back_kept[steps:] + came[steps:].astype(f32)).astype(bf16)
    near_part = grid.near_swap(near_part)

    grad_input, grad_blend, row_sums = call(
        blend_grad_kernel,
        "blend_backward",
        [
            ((steps, width), f32),
            ((steps, 2 * width), bf16),
            ((3, width), f32),
        ],
        [
            place,
            row_in,
            row_seed,
            back_kept,
            came,
            near_part,
            hidden_pre,
            update,
            hat,
            post_scale,
            line_of(later_normalizer_gain),
            spread,
        ],
        1,
    )
    (m_a, m_b) = moving
    m_a.value, m_b.parts, grad_blend = tie((m_a.value, m_b.parts, grad_blend))
    m_a.along()
    m_b.across()
    hidden_pieces = group(grad_blend)
    down = gathered(down_kept, down_sent)

    held = (m_a.value, m_b.value, hidden_pieces)
    m_a.value, m_b.value, hidden_pieces = tie(held)
    m_b.along()

    grad_reset, grad_value, probs_kept, probs_sent, span_sums = call(
        attention_grad_kernel,
        "attention_backward",
        [
            ((tokens, span), bf16),
            ((tokens, span), bf16),
            ((2 * steps, SPAN), f32),
            ((2 * steps, SPAN), f32),
            ((2, span), f32),
        ],
        [*hidden_pieces, reset_pre, attended, value, value_pre, probs_low, *w_second],
    )
    parts = weight_grad(
        grid,
        "reset_weights",
        width,
        (((0, 1, 2, 3), 0, 8), ((4, 5, 6, 7), 0, 9)),
        [*pieces, *hidden_pieces, grad_reset, mixed],
    )
    moving.append(Moving(grid, parts))
    m_c = moving[2]
    m_c.across()
    probs_gathered = gathered(probs_kept, probs_sent, f32)
    grad_gates, in_kept, *in_sent = call(
        functools.partial(input_grad_kernel, blocks),
        "input_backward",
        [((tokens, half), bf16), ((2 * steps, 2 * width), f32)]
        + [((2 * steps, half), bf16)] * 4,
        [place, *hidden_pieces, grad_reset, grad_value, spread, *w_first, *w_second],
        1,
    )
    m_b.value, in_kept, in_sent, down = tie((m_b.value, in_kept, in_sent, down))
    in_came = [swap(p) for p in in_sent]
    in_near = in_kept[steps:] + jnp.concatenate([p[steps:] for p in in_came], axis=1).astype(f32)
    in_near = grid.near_swap(in_near.astype(bf16))
    in_gathered = [in_kept, *in_came, in_near]
    grad_shared, narrow = call(
        score_grad_kernel,
        "scores_backward",
        [((steps, LANES), bf16), ((4, LANES), f32)],
        [*probs_gathered, probs, query, key, shared_pre, line_of(asking_gain), line_of(lookup_gain)],
    )
    parts = weight_grad(
        grid,
        "value_weights",
        width,
        (((0, 1, 2, 3), width, 4), ((0, 1, 2, 3), 0, 5), ((0,), 0, 6)),
        [*pieces, grad_value, grad_gates, grad_shared],
    )
    moving.append(Moving(grid, parts))
    m_d = moving[3]
    held = (m_c.value, m_d.parts, m_a.value, in_gathered)
    m_c.value, m_d.parts, m_a.value, in_gathered = tie(held)
    m_c.along()
    m_d.across()
    averages = call(
        ema_backward_kernel,
        "average_backward",
        [
            ((steps, width), bf16),
            ((steps, width), bf16),
            ((states + 8, width), f32),
            ((states + 8, width), f32),
        ],
        [
            place,
            row_in,
            gain,
            direct,
            params,
            spread,
            table,
            normed,
            pre,
            *in_gathered,
            grad_shared,
            grad_input,
            row_sums,
            seed_sum,
            narrow,
            *down,
            blended,
            line_of(outward_layer_offset),
            *w_first,
        ],
        1,
        [
            pltpu.VMEM((steps, width), f32),
            pltpu.VMEM((steps, width), f32),
            pltpu.VMEM((steps, width // LANES, LANES), f32),
        ],
    )
    sides = [m_a.near(), m_b.near()]
    held = (m_c.value, m_d.value, averages, sides)
    m_c.value, m_d.value, averages, sides = tie(held)
    m_d.along()
    grad_row, out_row, keep_rows, send_rows = averages

    lanes = COMMON_SPAN_DIM
    keep_rows = keep_rows + swap(send_rows)
    kept = keep_rows.shape[0]

    def placed(value):
        return near_order(value, jnp.zeros_like(value), 0).reshape(-1, width)

    wide_sums = [
        placed(span_sums[0]),
        placed(span_sums[1]),
        placed(jnp.concatenate(bffnin)),
    ]
    small = jnp.concatenate([keep_rows] + wide_sums, axis=0)
    sums = grid.sum_all(small)
    first_rows = sums[:kept]
    whole = in_order(first_rows, swap(sums)[:kept], 0)
    wide = sums[kept:]
    zero = whole[:states].T
    first = whole[kept : kept + states].T
    rate = jax.nn.sigmoid(inflow_logits)
    damp = jax.nn.sigmoid(decay_logits)
    grad_collapse = rate * channel_lifting * zero
    grad_inflow = channel_collapse * zero
    grad_keep = channel_collapse * rate * channel_lifting * first
    grad_lifting = grad_inflow * rate
    grad_rate = (grad_inflow * channel_lifting - grad_keep * damp) * rate * (1.0 - rate)
    grad_damp = -grad_keep * rate * damp * (1.0 - damp)
    rest = whole[states:]
    thin = rest[6].reshape(-1, lanes)

    (own_a, near_a), (own_b, near_b) = sides
    own_c, near_c = m_c.near()
    own_d, near_value, near_d = m_d.near((span,))
    out_in = near_order(
        jnp.concatenate([own_a[:, :ff], own_b[:, :ff]], axis=1),
        jnp.concatenate([near_a[:, :ff], near_b[:, :ff]], axis=1),
        1,
    )
    out_down = near_order(
        jnp.concatenate([own_a[:, ff:], own_b[:, ff:]], axis=1),
        jnp.concatenate([near_a[:, ff:], near_b[:, ff:]], axis=1),
        1,
    )
    out_reset = near_order(own_c[:, :span], near_c[:, :span], 1)
    out_wout = near_order(own_c[:, span:], near_c[:, span:], 1)
    out_value = near_order(own_d[:, :span], near_value, 1)
    own_d = own_d[:, span:]
    update_half = near_order(own_d[:, :quarter], near_d[:, :quarter], 1)
    hidden_half = near_order(own_d[:, quarter:half], near_d[:, quarter:half], 1)
    shared_half = own_d[:, half:] + near_d[:, half:]
    out_update = in_order(update_half, swap(update_half), 1)
    out_hidden = in_order(hidden_half, swap(hidden_half), 1)
    out_shared = shared_half + swap(shared_half)

    rows_out = jnp.stack([out_row, grad_row])
    rows_other = swap(rows_out)
    outputs = in_order(rows_out[:1], rows_other[:1], 0)
    grad_tokens = in_order(rows_out[1:], rows_other[1:], 0)
    return (
        outputs,
        grad_tokens,
        rest[0],
        grad_rate,
        grad_damp,
        grad_lifting,
        grad_collapse,
        rest[1],
        out_value,
        wide[0],
        out_shared,
        thin[0],
        thin[1],
        thin[2],
        thin[3],
        out_reset,
        wide[1],
        out_update,
        rest[2],
        out_hidden,
        rest[3],
        out_wout.T,
        rest[4],
        out_in,
        wide[2:].reshape(-1),
        out_down.T,
        rest[5],
    )


def solution(mesh):
    grid = Grid(mesh.shape["dp"])
    return jax.shard_map(
        functools.partial(per_device, grid),
        mesh=mesh,
        in_specs=(
            P(None, "dp", None),
            P(None, "dp", None),
            P(None, "dp"),
            P(),
            P(),
            P(),
            P(),
            P(),
            P(),
            P("dp", "mp"),
            P("mp"),
            P("dp", None),
            P(),
            P(),
            P(),
            P(),
            P("dp", "mp"),
            P("mp"),
            P("dp", None),
            P(),
            P("dp", None),
            P(),
            P("mp", "dp"),
            P(),
            P("dp", "mp"),
            P("mp"),
            P("mp", "dp"),
            P(),
        ),
        out_specs=(
            P(None, "dp", None),
            P(None, "dp", None),
            P(),
            P(),
            P(),
            P(),
            P(),
            P(),
            P("dp", "mp"),
            P("mp"),
            P("dp", None),
            P(),
            P(),
            P(),
            P(),
            P("dp", "mp"),
            P("mp"),
            P("dp", None),
            P(),
            P("dp", None),
            P(),
            P("mp", "dp"),
            P(),
            P("dp", "mp"),
            P("mp"),
            P("mp", "dp"),
            P(),
        ),
        check_vma=False,
    )
```

```python
import functools

import jax
import jax.numpy as jnp
from jax import lax
from jax.experimental import pallas as pl
from jax.experimental.pallas import tpu as pltpu
from jax.sharding import PartitionSpec as P

COMMON_SPAN_DIM = 128
SPAN = 128
LANES = 128
SUBLANES = 8

epsilon = 1e-05
bf16 = jnp.bfloat16
f32 = jnp.float32


def product(left, right):
    return jnp.dot(left, right, preferred_element_type=f32)


def left_inner(left, right):
    return lax.dot_general(left, right, (((0,), (0,)), ((), ())), preferred_element_type=f32)


def right_inner(left, right):
    return lax.dot_general(left, right, (((1,), (1,)), ((), ())), preferred_element_type=f32)


def silu_slope(values):
    sigma = jax.nn.sigmoid(values)
    return sigma * (1.0 + values * (1.0 - sigma))


def radices_of(n):
    found = []
    left = n // 2
    while left > 1:
        r = 4 if left % 4 == 0 or not found and left > 4 else 2
        r = r if left % r == 0 else left
        found.append(r)
        left //= r
    while len(found) < 2:
        found.append(1)
    return tuple(found) + (2,)


class Grid:
    def __init__(self, n):
        self.n = n
        radix = radices_of(n)
        strides, left = [], n
        for r in radix:
            left //= r
            strides.append(left)
        self.radix = radix[1:-1] + radix[:1] + radix[-1:]
        self.stride = tuple(strides[1:-1] + strides[:1] + strides[-1:])
        self.near = len(radix) - 1
        self.line = len(radix) - 2

    def shift(self, dim, k):
        pairs = []
        for source in range(self.n):
            at = (source // self.stride[dim]) % self.radix[dim]
            to = (at + k) % self.radix[dim]
            pairs.append((source, source + (to - at) * self.stride[dim]))
        return pairs

    def fetch(self, array, dim):
        return [array] + [
            lax.ppermute(array, "dp", self.shift(dim, -k)) for k in range(1, self.radix[dim])
        ]

    def deliver(self, parts, dim):
        return [parts[0]] + [
            lax.ppermute(parts[k], "dp", self.shift(dim, k)) for k in range(1, self.radix[dim])
        ]

    def near_index(self):
        return lax.axis_index("dp") % 2

    def near_swap(self, value):
        return lax.ppermute(value, "dp", self.shift(self.near, 1))

    def sum_all(self, value):
        for dim in [self.near, *range(self.line), self.line]:
            r = self.radix[dim]
            got = self.fetch(value.astype(bf16) if dim == self.line else value, dim)
            got = [g.astype(f32) for g in got]
            if r == 4:
                value = (got[0] + got[2]) + (got[1] + got[3])
            elif r == 2:
                value = got[0] + got[1]
            elif r > 2:
                value = lax.psum(value, "dp", axis_index_groups=self.groups(dim))
        return value

    def groups(self, dim):
        lines = {}
        for i in range(self.n):
            at = (i // self.stride[dim]) % self.radix[dim]
            lines.setdefault(i - at * self.stride[dim], []).append(i)
        return list(lines.values())

    def permutation(self, width):
        rows = width // self.n
        me = lax.axis_index("dp")
        place = jnp.arange(width)
        block = place // rows
        absolute = place % rows + (block % 2) * rows
        block = block // 2
        for s, r in list(zip(self.stride, self.radix))[-2::-1]:
            absolute = absolute + ((block % r + (me // s) % r) % r) * (s * rows)
            block = block // r
        return (jnp.arange(width)[:, None] == absolute[None, :]).astype(bf16)


def total_of(parts):
    total = parts[0].astype(f32)
    for p in parts[1:]:
        total = total + p.astype(f32)
    return total


def tie(values):
    return lax.optimization_barrier(values)


class Gather:
    def __init__(self, grid, mine, theirs, held):
        self.grid = grid
        near = grid.near_index()
        pack = functools.partial(jnp.concatenate, axis=1)
        kept = [pack(chunk) for chunk in mine]
        sent = [pack(chunk) for chunk in theirs]

        def beside(own, other):
            return jnp.stack([jnp.where(near == 0, own, other), jnp.where(near == 0, other, own)])

        first = beside(kept[0], grid.near_swap(sent[0]))
        rest = pack(sent[1:])
        first, rest, self.held = tie((first, rest, held))
        rest = grid.near_swap(rest)
        self.state, at = [first], 0
        for own in kept[1:]:
            self.state.append(beside(own, rest[:, at : at + own.shape[1]]))
            at += own.shape[1]
        self.middle = list(range(grid.line - 1, -1, -1))
        self.weights = {}
        self.stage = 0

    def advance(self, held=None):
        stage, count = self.stage, len(self.state)
        active = [k for k in range(count) if 0 <= stage - k <= len(self.middle)]
        last = stage - 1 - len(self.middle)
        done = self.weights[last] if last in self.weights else []
        if stage:
            tied, done, held = tie(([self.state[k] for k in active], done, held))
            for k, value in zip(active, tied):
                self.state[k] = value
            if last in self.weights:
                self.weights[last] = done
        for k in active:
            step = stage - k
            dim = self.grid.line if step == 0 else self.middle[step - 1]
            got = self.grid.fetch(self.state[k], dim)
            if step < len(self.middle):
                self.state[k] = jnp.stack(got)
            else:
                self.weights[k] = [g.reshape(-1, g.shape[-1]) for g in got]
        self.stage += 1
        return held

    def until(self, k):
        while k not in self.weights:
            self.advance()


class Moving:
    def __init__(self, grid, parts):
        self.grid = grid
        shape = grid.radix[1:] + (-1, parts[0].shape[-1])
        self.parts = [p.reshape(shape) for p in parts]
        self.value = None

    def across(self):
        self.value = total_of(self.grid.deliver(self.parts, 0))
        for dim in range(1, self.grid.line):
            value = self.value.astype(bf16)
            self.value = total_of(
                self.grid.deliver([value[k] for k in range(self.grid.radix[dim])], dim)
            )
        self.value = self.value.astype(bf16)

    def along(self):
        parts = [self.value[k] for k in range(self.grid.radix[self.grid.line])]
        self.value = total_of(self.grid.deliver(parts, self.grid.line))

    def near(self, cuts=()):
        near = self.grid.near_index()
        kept = lax.dynamic_index_in_dim(self.value, near, 0, keepdims=False)
        sent = lax.dynamic_index_in_dim(self.value, 1 - near, 0, keepdims=False)
        edges = [0, *cuts, sent.shape[1]]
        came = [
            self.grid.near_swap(sent[:, a:b].astype(bf16)).astype(f32)
            for a, b in zip(edges, edges[1:])
        ]
        return (kept, *came)


def tiles_of(array):
    return [array[i * SUBLANES : (i + 1) * SUBLANES] for i in range(array.shape[0] // SUBLANES)]


def row_tile(table_ref, lag, c):
    row = table_ref[lag, pl.ds(c, 1), :]
    return jnp.broadcast_to(row, (SUBLANES, LANES))


def norm_parts(x_ref):
    values = x_ref[...].astype(f32)
    center = values - jnp.mean(values, axis=-1, keepdims=True)
    scale = lax.rsqrt(jnp.mean(center * center, axis=-1, keepdims=True) + epsilon)
    return center * scale, scale


def sigma_of(values):
    return jax.nn.sigmoid(values)


def call(kernel, name, out, operands, scalars=0, scratch=()):
    specs = [pl.BlockSpec(memory_space=pltpu.SMEM)] * scalars
    specs += [pl.BlockSpec(memory_space=pltpu.VMEM)] * (len(operands) - scalars)
    return pl.pallas_call(
        kernel,
        name=name,
        out_shape=[jax.ShapeDtypeStruct(shape, dtype) for shape, dtype in out],
        in_specs=specs,
        out_specs=[pl.BlockSpec(memory_space=pltpu.VMEM)] * len(out),
        scratch_shapes=list(scratch),
        cost_estimate=pl.CostEstimate(flops=1, bytes_accessed=1, transcendentals=0),
    )(*operands)


def times(x, blocks, start, stop):
    total, at = None, 0
    for w in blocks:
        rows = w.shape[0]
        term = product(x[:, at : at + rows], w[:, start:stop])
        total = term if total is None else total + term
        at += rows
    return total


def times_t(x, blocks, start, stop):
    return jnp.concatenate([right_inner(x, w[:, start:stop]) for w in blocks], axis=1)


def two_terms(value):
    high = value.astype(bf16)
    return [high, (value - high.astype(f32)).astype(bf16)]


def to_absolute(value, spread):
    rows = value.shape[0]
    out = right_inner(jnp.concatenate(two_terms(value), axis=0), spread)
    return out[:rows] + out[rows:]


def column_sum(values):
    return jnp.sum(values, axis=0, keepdims=True)


def ema_forward_kernel(
    place_ref, x_ref, seed_ref, gain_ref, direct_ref, params_ref, spread_ref,
    normed_ref, pre_ref, packed_ref, seed_low_ref, table_ref, seed_sum_ref,
):
    steps, width = x_ref.shape
    spread = spread_ref[...]
    hat, unused = norm_parts(x_ref)
    normed = hat * gain_ref[...]
    normed_ref[...] = normed
    live = lax.broadcasted_iota(jnp.int32, (steps, 1), 0) < place_ref[2]
    seed = jnp.where(live, seed_ref[...].astype(f32), 0.0)
    seed_sum_ref[...] = column_sum(seed)
    rate = jax.nn.sigmoid(params_ref[0])
    keep = 1.0 - rate * jax.nn.sigmoid(params_ref[1])
    weight = params_ref[3] * (rate * params_ref[2])

    def lag_step(lag, power):
        table_ref[lag] = jnp.sum(weight * power, axis=0)
        return power * keep

    lax.fori_loop(0, steps, lag_step, jnp.ones_like(keep))
    count = steps // SUBLANES
    sub = lax.broadcasted_iota(jnp.int32, (steps, LANES), 0)

    def block(c, carry):
        columns = pl.ds(pl.multiple_of(c * LANES, LANES), LANES)
        base = normed_ref[:, columns]
        total = [jnp.zeros((SUBLANES, LANES), f32)] * count
        for r in range(SUBLANES):
            moved = base if r == 0 else jnp.where(sub >= r, pltpu.roll(base, r, 0), 0.0)
            moved = tiles_of(moved)
            for q in range(count):
                w = row_tile(table_ref, q * SUBLANES + r, c)
                for i in range(q, count):
                    total[i] = total[i] + w * moved[i - q]
        pre_ref[:, columns] = jnp.concatenate(total, axis=0) + direct_ref[:, columns] * base
        return carry

    lax.fori_loop(0, width // LANES, block, 0)
    pre = pre_ref[...]
    smooth = (pre * jax.nn.sigmoid(pre)).astype(bf16)
    rows = jnp.concatenate([smooth, normed_ref[...].astype(bf16), seed.astype(bf16)], axis=0)
    rows = product(rows, spread).astype(bf16)
    packed_ref[:, :width] = rows[:steps]
    packed_ref[:, width:] = rows[steps : 2 * steps]
    seed_low_ref[...] = rows[2 * steps :]


def ema_backward_kernel(
    place_ref,
    x_ref, gain_ref, direct_ref, params_ref, spread_ref, table_ref, normed_ref, pre_ref,
    kept_ref, core_0, core_1, core_2, core_3, near_ref,
    grad_shared_ref, grad_input_ref, row_sums_ref, seed_sum_ref,
    narrow_ref, down_kept_ref, down_core_ref, down_near_ref, blended_ref, offset_ref, *rest,
):
    weights = rest[:-7]
    grad_row_ref, out_row_ref, keep_ref, send_ref, smooth_ref, inner_ref, lag_ref = rest[-7:]
    vectors_ref = send_ref
    steps, width = x_ref.shape
    count = steps // SUBLANES
    sub = lax.broadcasted_iota(jnp.int32, (steps, LANES), 0)
    spread = spread_ref[...]

    down = down_kept_ref[:steps] + down_core_ref[:steps].astype(f32) + down_near_ref[...].astype(f32)
    core = [p[:steps].astype(f32) for p in (core_0, core_1, core_2, core_3)]
    sums = kept_ref[:steps] + jnp.concatenate(core, axis=1) + near_ref[...].astype(f32)
    smooth, norm = sums[:, :width], sums[:, width:]
    span = weights[0].shape[1] - LANES
    smooth = smooth + times_t(grad_shared_ref[...], weights, span, span + LANES)
    terms = [down.astype(bf16), *two_terms(smooth), *two_terms(norm)]
    out = right_inner(jnp.concatenate(terms, axis=0), spread)
    smooth_ref[...] = out[steps : 2 * steps] + out[2 * steps : 3 * steps]
    inner_ref[...] = out[3 * steps : 4 * steps] + out[4 * steps :]
    live = lax.broadcasted_iota(jnp.int32, (steps, 1), 0) < place_ref[2]
    out_row = blended_ref[...] + out[:steps] + offset_ref[...]
    out_row_ref[...] = jnp.where(live, out_row, 0.0).astype(bf16)

    def block(c, carry):
        columns = pl.ds(pl.multiple_of(c * LANES, LANES), LANES)
        pre = pre_ref[:, columns]
        grad_pre = smooth_ref[:, columns] * silu_slope(pre)
        normed = normed_ref[:, columns]
        vectors_ref[1:2, columns] = column_sum(grad_pre * normed)
        own = tiles_of(normed)
        total = tiles_of(inner_ref[:, columns] + direct_ref[:, columns] * grad_pre)
        for r in range(SUBLANES):
            moved = grad_pre
            if r:
                moved = jnp.where(sub < steps - r, pltpu.roll(grad_pre, steps - r, 0), 0.0)
            moved = tiles_of(moved)
            for q in range(count):
                w = row_tile(table_ref, q * SUBLANES + r, c)
                lag_sum = jnp.zeros((SUBLANES, LANES), f32)
                for i in range(count - q):
                    g = moved[i + q]
                    total[i] = total[i] + w * g
                    lag_sum = lag_sum + g * own[i]
                lag_ref[q * SUBLANES + r, pl.ds(c, 1), :] = column_sum(lag_sum)
        inner_ref[:, columns] = jnp.concatenate(total, axis=0)
        return carry

    lax.fori_loop(0, width // LANES, block, 0)

    keep_all = 1.0 - jax.nn.sigmoid(params_ref[0]) * jax.nn.sigmoid(params_ref[1])
    states = keep_all.shape[0]
    half = states // 2
    sums_of_lags = [[], []]
    for h in range(2):
        keep = keep_all[h * half : (h + 1) * half]

        def lag_step(lag, carry):
            power, zero, first = carry
            g = lag_ref[lag]
            first = first + (g * lag.astype(f32))[None] * power
            power = power * keep
            return (power, zero + g[None] * power, first)

        blank = jnp.zeros_like(keep)
        start = (jnp.ones_like(keep), blank + lag_ref[0][None], blank)
        unused, zero, first = lax.fori_loop(1, steps, lag_step, start)
        sums_of_lags[0].append(zero)
        sums_of_lags[1].append(first)

    hat, scale = norm_parts(x_ref)
    grad = inner_ref[...]
    prenorm = column_sum(grad * hat)
    grad = grad * gain_ref[...]
    grad = grad - jnp.mean(grad, axis=-1, keepdims=True) - hat * jnp.mean(
        grad * hat, axis=-1, keepdims=True
    )
    grad_row_ref[...] = (grad_input_ref[...] + scale * grad).astype(bf16)

    def flat(states_first):
        blocks = range(width // LANES)
        return jnp.concatenate([states_first[:, c] for c in blocks], axis=1)

    zero, first = [flat(jnp.concatenate(part, axis=0)) for part in sums_of_lags]
    narrow = jnp.concatenate([narrow_ref[k : k + 1] for k in range(4)], axis=1)
    narrow = jnp.concatenate([narrow, jnp.zeros((1, width - narrow.shape[1]), f32)], axis=1)
    rest_rows = [prenorm, vectors_ref[1:2], row_sums_ref[...], seed_sum_ref[...], narrow]
    rest_rows = jnp.concatenate(rest_rows + [jnp.zeros((1, width), f32)], axis=0)
    keep, send = pick(place_ref[1], zero, first)
    keep_rest, send_rest = pick(place_ref[1], rest_rows, jnp.zeros_like(rest_rows))
    keep_ref[:states] = keep
    keep_ref[states:] = keep_rest
    send_ref[:states] = send
    send_ref[states:] = send_rest


def attention_kernel(
    place_ref, p0, p1, p2, p3, value_offset_ref, common_offset_ref, ask_gain_ref, ask_offset_ref,
    look_gain_ref, *rest,
):
    weights = rest[:-11]
    (
        value_pre_ref, value_ref, gates_ref, gates_core_ref, gates_near_ref, probs_low_ref,
        attended_ref, shared_pre_ref, query_ref, key_ref, probs_ref,
    ) = rest[-11:]
    steps = p0.shape[0]
    width = p0.shape[1] // 2
    span = value_ref.shape[1]
    gates_size = gates_ref.shape[1]
    at = lax.broadcasted_iota(jnp.int32, (steps, steps), 0)
    to = lax.broadcasted_iota(jnp.int32, (steps, steps), 1)
    pieces = (p0, p1, p2, p3)
    smooth = jnp.concatenate([p[:, :width] for p in pieces], axis=0)
    norm = jnp.concatenate([p[:, width:] for p in pieces], axis=0)
    value_pre = times(norm, weights, 0, span) + value_offset_ref[...]
    value_pre_ref[...] = value_pre
    value_ref[...] = (value_pre * sigma_of(value_pre)).astype(bf16)
    gates = times(smooth, weights, span, span + gates_size)
    gates_ref[...] = gates[:steps]
    gates_core_ref[...] = gates[2 * steps : 3 * steps]
    gates_near_ref[:steps] = gates[steps : 2 * steps].astype(bf16)
    gates_near_ref[steps:] = gates[3 * steps :].astype(bf16)
    start = span + gates_size
    shared_pre = times(smooth, weights, start, start + LANES) + common_offset_ref[...]
    shared = shared_pre * sigma_of(shared_pre)
    query = (shared * ask_gain_ref[...] + ask_offset_ref[...]).astype(bf16)
    key = (shared * look_gain_ref[...]).astype(bf16)
    shared_pre_ref[...] = shared_pre[:steps]
    query_ref[...] = query[:steps]
    key_ref[...] = key[:steps]
    for p in range(4):
        here = slice(p * steps, (p + 1) * steps)
        scores = right_inner(query[here], key[here]) * (COMMON_SPAN_DIM ** (-0.5))
        allowed = (to <= at) & ((to < place_ref[2 + p]) | (to == at))
        scores = jnp.where(allowed, scores, -1e30)
        probs = jnp.exp(scores - jnp.max(scores, axis=-1, keepdims=True))
        probs = probs / jnp.sum(probs, axis=-1, keepdims=True)
        probs_low = probs.astype(bf16)
        probs_low_ref[here] = probs_low
        attended_ref[here] = product(probs_low, value_ref[here])
        if p == 0:
            probs_ref[...] = probs


def mix_kernel(p0, p1, p2, p3, offset_ref, attended_ref, *rest):
    weights = rest[:-4]
    reset_pre_ref, mixed_ref, kept_ref, sent_ref = rest[-4:]
    steps = p0.shape[0]
    width = p0.shape[1] // 2
    span = mixed_ref.shape[1]
    smooth = jnp.concatenate([p[:, :width] for p in (p0, p1, p2, p3)], axis=0)
    reset_pre = times(smooth, weights, 0, span) + offset_ref[...]
    reset_pre_ref[...] = reset_pre
    mixed = (reset_pre * sigma_of(reset_pre) * attended_ref[...]).astype(bf16)
    mixed_ref[...] = mixed
    part = times_t(mixed, weights, span, 2 * span)
    kept_ref[...] = part[: 2 * steps]
    sent_ref[...] = part[2 * steps :].astype(bf16)


def pick(index, own, other):
    zero = index == 0
    return [jnp.where(zero, own, other), jnp.where(zero, other, own)]


def hidden_kernel(
    place_ref, x_ref, kept_ref, core_ref, near_ref,
    gates_ref, gates_core_ref, gates_near_ref, gates_far_ref,
    update_offset_ref, hidden_offset_ref, gain_ref, spread_ref,
    hidden_pre_ref, update_ref, blended_ref, hat_ref, scale_ref, low_ref,
):
    steps = x_ref.shape[0]
    spread = spread_ref[...]
    part = kept_ref[:steps] + core_ref[:steps].astype(f32) + near_ref[...].astype(f32)
    size = gates_ref.shape[1] // 2
    sides = []
    for own, other in (
        (gates_ref[...], gates_near_ref[:steps].astype(f32)),
        (gates_core_ref[...], gates_far_ref[...].astype(f32)),
    ):
        sides.append(
            [
                jnp.concatenate(
                    pick(place_ref[0], own[:, k * size : (k + 1) * size], other[:, k * size : (k + 1) * size]),
                    axis=1,
                )
                for k in range(2)
            ]
        )
    whole = [jnp.concatenate(pick(place_ref[1], sides[0][k], sides[1][k]), axis=1) for k in range(2)]
    update = sigma_of(whole[0] + update_offset_ref[...])
    hidden_pre = whole[1] + hidden_offset_ref[...] + to_absolute(part, spread)
    hidden = hidden_pre * sigma_of(hidden_pre)
    values = x_ref[...].astype(f32)
    blended = values + update * (hidden - values)
    center = blended - jnp.mean(blended, axis=-1, keepdims=True)
    scale = lax.rsqrt(jnp.mean(center * center, axis=-1, keepdims=True) + epsilon)
    hat = center * scale
    hidden_pre_ref[...] = hidden_pre
    update_ref[...] = update
    blended_ref[...] = blended
    hat_ref[...] = hat
    scale_ref[...] = scale
    low_ref[...] = product((hat * gain_ref[...]).astype(bf16), spread).astype(bf16)


def ffn_kernel(first, count, *refs):
    f = refs[:4]
    seeds = refs[4:8]
    offset_ref = refs[8]
    at = 9
    if not first:
        down_before_ref, back_before_ref = refs[9:11]
        at = 11
    weights = refs[at : at + count]
    outs = refs[at + count :]
    grad_pre_ref, act_ref, bias_ref = outs[:3]
    steps = f[0].shape[0]
    span = act_ref.shape[1]
    pre = times(jnp.concatenate([p[...] for p in f], axis=0), weights, 0, span) + offset_ref[...]
    sigma = sigma_of(pre)
    act = (pre * sigma).astype(bf16)
    act_ref[...] = act
    seed = jnp.concatenate([p[...] for p in seeds], axis=0)
    grad = times(seed, weights, span, 2 * span)
    grad = (grad * (sigma * (1.0 + pre * (1.0 - sigma)))).astype(bf16)
    grad_pre_ref[...] = grad
    bias_ref[...] = column_sum(grad.astype(f32))
    down = times_t(act, weights, span, 2 * span)
    back = times_t(grad, weights, 0, span)
    if first:
        down_ref, back_ref = outs[3:5]
        down_ref[...] = down
        back_ref[...] = back
        return
    down_kept_ref, down_sent_ref, back_kept_ref, back_sent_ref = outs[3:7]
    down = down + down_before_ref[...]
    down_kept_ref[...] = down[: 2 * steps]
    down_sent_ref[...] = down[2 * steps :].astype(bf16)
    back = back + back_before_ref[...]
    back_kept_ref[...] = back[: 2 * steps]
    back_sent_ref[...] = back[2 * steps :].astype(bf16)


def blend_grad_kernel(
    place_ref, x_ref, seed_ref, kept_ref, core_ref, near_ref, hidden_pre_ref, update_ref, hat_ref,
    scale_ref, gain_ref, spread_ref,
    grad_input_ref, packed_ref, sums_ref,
):
    steps, width = x_ref.shape
    spread = spread_ref[...]
    part = kept_ref[:steps] + core_ref[:steps].astype(f32) + near_ref[...].astype(f32)
    grad_norm = to_absolute(part, spread)
    hat = hat_ref[...]
    grad_hat = grad_norm * gain_ref[...]
    live = lax.broadcasted_iota(jnp.int32, (steps, 1), 0) < place_ref[2]
    seed = jnp.where(live, seed_ref[...].astype(f32), 0.0)
    grad_blended = seed + scale_ref[...] * (
        grad_hat
        - jnp.mean(grad_hat, axis=-1, keepdims=True)
        - hat * jnp.mean(grad_hat * hat, axis=-1, keepdims=True)
    )
    update = update_ref[...]
    hidden_pre = hidden_pre_ref[...]
    sigma = sigma_of(hidden_pre)
    values = x_ref[...].astype(f32)
    grad_input_ref[...] = grad_blended * (1.0 - update)
    grad_hidden = (
        grad_blended * update * (sigma * (1.0 + hidden_pre * (1.0 - sigma)))
    ).astype(bf16)
    grad_update = (
        grad_blended * (hidden_pre * sigma - values) * update * (1.0 - update)
    ).astype(bf16)
    packed_ref[:, :width] = product(grad_hidden, spread).astype(bf16)
    packed_ref[:, width:] = grad_update
    sums_ref[0:1] = column_sum(grad_update.astype(f32))
    sums_ref[1:2] = column_sum(grad_hidden.astype(f32))
    sums_ref[2:3] = column_sum(grad_norm * hat)


def attention_grad_kernel(
    h0, h1, h2, h3, reset_pre_ref, attended_ref, value_ref, value_pre_ref, probs_low_ref, *rest,
):
    weights = rest[:-5]
    grad_reset_ref, grad_value_ref, kept_ref, sent_ref, sums_ref = rest[-5:]
    steps = h0.shape[0]
    span = value_ref.shape[1]
    grad_mixed = times(
        jnp.concatenate([h[:, : h.shape[1] // 2] for h in (h0, h1, h2, h3)], axis=0),
        weights,
        span,
        2 * span,
    )
    reset_pre = reset_pre_ref[...]
    sigma = sigma_of(reset_pre)
    grad_attended = (grad_mixed * (reset_pre * sigma)).astype(bf16)
    grad_reset = (
        grad_mixed * attended_ref[...] * (sigma * (1.0 + reset_pre * (1.0 - sigma)))
    ).astype(bf16)
    grad_reset_ref[...] = grad_reset
    sums_ref[1:2] = column_sum(grad_reset.astype(f32))
    for p in range(4):
        here = slice(p * steps, (p + 1) * steps)
        part = right_inner(grad_attended[here], value_ref[here])
        half = slice((p % 2) * steps, (p % 2 + 1) * steps)
        if p < 2:
            kept_ref[half] = part
        else:
            sent_ref[half] = part
        grad_value = left_inner(probs_low_ref[here], grad_attended[here])
        grad_value = (grad_value * silu_slope(value_pre_ref[here])).astype(bf16)
        grad_value_ref[here] = grad_value
        term = column_sum(grad_value.astype(f32))
        sums_ref[0:1] = term if p == 0 else sums_ref[0:1] + term


def input_grad_kernel(count, place_ref, *refs):
    h = refs[:4]
    grad_reset_ref, grad_value_ref, spread_ref = refs[4:7]
    first = refs[7 : 7 + count]
    second = refs[7 + count : 7 + 2 * count]
    gates_ref, kept_ref, *sent = refs[7 + 2 * count :]
    steps = h[0].shape[0]
    width = h[0].shape[1] // 2
    span = grad_value_ref.shape[1]
    size = gates_ref.shape[1] // 2
    gate = pl.ds(pl.multiple_of(place_ref[6], size), size)
    rows = spread_ref[gate, :]
    late = pl.ds(pl.multiple_of(width + place_ref[6], size), size)
    update = jnp.concatenate([p[:, late] for p in h], axis=0)
    hidden = right_inner(jnp.concatenate([p[:, :width] for p in h], axis=0), rows).astype(bf16)
    gates = jnp.concatenate([update, hidden], axis=1)
    gates_ref[...] = gates
    smooth = times_t(grad_reset_ref[...], second, 0, span) + times_t(
        gates, first, span, span + 2 * size
    )
    norm = times_t(grad_value_ref[...], first, 0, span)
    kept_ref[:, :width] = smooth[: 2 * steps]
    kept_ref[:, width:] = norm[: 2 * steps]
    for k, out in enumerate(sent):
        part = (smooth, norm)[k // 2][2 * steps :]
        at = (k % 2) * out.shape[1]
        out[...] = part[:, at : at + out.shape[1]].astype(bf16)


def score_grad_kernel(
    kept_ref, core_ref, near_ref, probs_ref, query_ref, key_ref, shared_pre_ref, ask_gain_ref,
    look_gain_ref, grad_shared_ref, sums_ref,
):
    steps = probs_ref.shape[0]
    grad_probs = kept_ref[:steps] + core_ref[:steps] + near_ref[...]
    probs = probs_ref[...]
    grad_scores = (
        probs * (grad_probs - jnp.sum(grad_probs * probs, axis=-1, keepdims=True))
    ).astype(bf16)
    scale = COMMON_SPAN_DIM ** (-0.5)
    grad_query = product(grad_scores, key_ref[...]) * scale
    grad_key = left_inner(grad_scores, query_ref[...]) * scale
    shared_pre = shared_pre_ref[...]
    sigma = sigma_of(shared_pre)
    shared = shared_pre * sigma
    grad_shared = (
        (grad_query * ask_gain_ref[...] + grad_key * look_gain_ref[...])
        * (sigma * (1.0 + shared_pre * (1.0 - sigma)))
    ).astype(bf16)
    grad_shared_ref[...] = grad_shared
    sums_ref[0:1] = column_sum(grad_shared.astype(f32))
    sums_ref[1:2] = column_sum(grad_query * shared)
    sums_ref[2:3] = column_sum(grad_query)
    sums_ref[3:4] = column_sum(grad_key * shared)


def weight_grad_kernel(plan, count, *refs):
    outs = refs[len(refs) - count :]
    at = 0
    for lefts, start, right in plan:
        columns = refs[right].shape[1]
        for k, out in enumerate(outs):
            size = out.shape[0]
            cut = slice(start + k * size, start + (k + 1) * size)
            left = jnp.concatenate([refs[i][:, cut] for i in lefts], axis=0)
            out[:, at : at + columns] = left_inner(left, refs[right][...]).astype(bf16)
        at += columns


def weight_grad(grid, name, width, plan, operands):
    count = grid.radix[0]
    columns = sum(operands[right].shape[1] for unused, start, right in plan)
    return call(
        functools.partial(weight_grad_kernel, plan, count),
        name,
        [((width // count, columns), bf16)] * count,
        operands,
    )


def per_device(
    grid,
    layer_entries,
    loss_sensitivity,
    occupied_counts,
    earlier_normalizer_gain,
    inflow_logits,
    decay_logits,
    channel_lifting,
    channel_collapse,
    direct_term_weight,
    content_projector,
    content_offset,
    common_projector,
    common_offset,
    asking_gain,
    asking_offset,
    lookup_gain,
    forget_gate_matrix,
    forget_gate_offset,
    renewal_gate_matrix,
    renewal_gate_offset,
    candidate_matrix,
    candidate_offset,
    attended_projector,
    later_normalizer_gain,
    hidden_layer_matrix,
    hidden_layer_offset,
    outward_layer_matrix,
    outward_layer_offset,
):
    core = lax.axis_index("mp")
    near = grid.near_index()
    micro, steps, width = layer_entries.shape
    half, quarter = width // 2, width // 4
    span = content_projector.shape[1] // 2
    ff = hidden_layer_matrix.shape[1] // 4
    swap_pairs = [(0, 1), (1, 0)]

    def swap(value):
        return lax.ppermute(value, "mp", swap_pairs)

    def group(own):
        near_own = grid.near_swap(own)
        return [own, near_own, swap(own), swap(near_own)]

    def gathered(kept, sent, near_type=bf16):
        came = swap(sent)
        rows = kept.shape[0] // 2
        near_part = (kept[rows:] + came[rows:].astype(f32)).astype(near_type)
        return kept, came, grid.near_swap(near_part)

    def ordered(index, own, other, axis):
        first = jnp.where(index == 0, own, other)
        second = jnp.where(index == 0, other, own)
        return jnp.concatenate([first, second], axis=axis)

    in_order = functools.partial(ordered, core)
    near_order = functools.partial(ordered, near)

    def cut(value, start, size, axis):
        return lax.dynamic_slice_in_dim(value, start, size, axis=axis)

    def chunks_of(side):
        gate = (2 * core + side) * quarter
        hidden = [side * 2 * ff, side * 2 * ff + ff]
        return [
            [
                cut(content_projector, side * span, span, 1),
                cut(renewal_gate_matrix, gate, quarter, 1),
                cut(candidate_matrix, gate, quarter, 1),
                common_projector,
            ],
            [
                cut(forget_gate_matrix, side * span, span, 1),
                cut(attended_projector, side * span, span, 0).T,
            ],
        ] + [
            [cut(hidden_layer_matrix, at, ff, 1), cut(outward_layer_matrix, at, ff, 0).T]
            for at in hidden
        ]

    held = (layer_entries, loss_sensitivity, occupied_counts)
    gather = Gather(grid, chunks_of(near), chunks_of(1 - near), held)
    layer_entries, loss_sensitivity, occupied_counts = gather.held
    gather.advance()

    row_in = lax.dynamic_index_in_dim(layer_entries, core, 0, keepdims=False)
    row_seed = lax.dynamic_index_in_dim(loss_sensitivity, core, 0, keepdims=False)
    counts = ordered(core, occupied_counts[:1, 0], occupied_counts[1:, 0], 0)
    near_counts = grid.near_swap(counts)
    gate = (2 * core + near) * quarter
    place = jnp.stack(
        [near, core, counts[0], near_counts[0], counts[1], near_counts[1], gate]
    ).astype(jnp.int32)
    spread = grid.permutation(width)
    params = jnp.concatenate(
        [inflow_logits, decay_logits, channel_lifting, channel_collapse], axis=1
    )
    states = inflow_logits.shape[1]
    params = params.T.reshape(4, states, width // LANES, LANES)

    def line_of(value):
        return value.reshape(1, -1)

    gain, direct = line_of(earlier_normalizer_gain), line_of(direct_term_weight)
    tokens = 4 * steps
    normed, pre, packed, seed_low, table, seed_sum = call(
        ema_forward_kernel,
        "average_forward",
        [
            ((steps, width), f32),
            ((steps, width), f32),
            ((steps, 2 * width), bf16),
            ((steps, width), bf16),
            ((steps, width // LANES, LANES), f32),
            ((1, width), f32),
        ],
        [place, row_in, row_seed, gain, direct, params, spread],
        1,
    )
    gather.until(0) if gather.middle[1:] else None
    packed = gather.advance(packed)
    pieces = group(packed)
    seed_low = gather.advance(seed_low)
    near_seed = grid.near_swap(seed_low)
    w_first = gather.weights[0]
    blocks = len(w_first)

    (
        value_pre, value, gates, gates_core, gates_near, probs_low, attended, shared_pre, query, key, probs
    ) = call(
        attention_kernel,
        "attention_forward",
        [
            ((tokens, span), f32),
            ((tokens, span), bf16),
            ((steps, half), f32),
            ((steps, half), f32),
            ((2 * steps, half), bf16),
            ((tokens, SPAN), bf16),
            ((tokens, span), f32),
            ((steps, LANES), f32),
            ((steps, LANES), bf16),
            ((steps, LANES), bf16),
            ((steps, SPAN), f32),
        ],
        [
            place,
            *pieces,
            line_of(cut(content_offset, near * span, span, 0)),
            line_of(common_offset),
            line_of(asking_gain),
            line_of(asking_offset),
            line_of(lookup_gain),
            *w_first,
        ],
        1,
    )
    attended, gates_near, gates_core, near_seed = gather.advance(
        (attended, gates_near, gates_core, near_seed)
    )
    seeds = [seed_low, near_seed, swap(seed_low), swap(near_seed)]
    gates_near = grid.near_swap(gates_near)
    w_second = gather.weights[1]
    reset_pre, mixed, mix_kept, mix_sent = call(
        mix_kernel,
        "reset_and_mix",
        [
            ((tokens, span), f32),
            ((tokens, span), bf16),
            ((2 * steps, width), f32),
            ((2 * steps, width), bf16),
        ],
        [*pieces, line_of(cut(forget_gate_offset, near * span, span, 0)), attended, *w_second],
    )
    mix_kept, mix_sent, gates_near = gather.advance((mix_kept, mix_sent, gates_near))
    mix_came = swap(mix_sent)
    mix_near = grid.near_swap((mix_kept[steps:] + mix_came[steps:].astype(f32)).astype(bf16))
    hidden_pre, update, blended, hat, post_scale, ffn_low = call(
        hidden_kernel,
        "hidden_and_norm",
        [((steps, width), f32)] * 4 + [((steps, 1), f32), ((steps, width), bf16)],
        [
            place,
            row_in,
            mix_kept,
            mix_came,
            mix_near,
            gates,
            swap(gates_core),
            gates_near,
            swap(gates_near[steps:]),
            line_of(renewal_gate_offset),
            line_of(candidate_offset),
            line_of(later_normalizer_gain),
            spread,
        ],
        1,
    )
    ffn_pieces = group(ffn_low)
    while gather.stage < len(gather.state) + len(gather.middle):
        gather.advance()

    ffn_offset = line_of(cut(hidden_layer_offset, near * 2 * ff, 2 * ff, 0))
    moving = []
    bffnin = []
    before = []
    for at in range(2):
        first = at == 0
        out = [((tokens, ff), bf16), ((tokens, ff), bf16), ((1, ff), f32)]
        if first:
            out += [((tokens, width), f32)] * 2
        else:
            out += [((2 * steps, width), f32), ((2 * steps, width), bf16)] * 2
        grad_pre, act, bias, *before = call(
            functools.partial(ffn_kernel, first, blocks),
            "feed_forward",
            out,
            [*ffn_pieces, *seeds, ffn_offset[:, at * ff : (at + 1) * ff], *before, *gather.weights[2 + at]],
        )
        bffnin.append(bias[0])
        if not first:
            down_kept, down_sent, back_kept, back_sent = before
            came = swap(back_sent)
        parts = weight_grad(
            grid,
            "feed_forward_weights",
            width,
            (((0, 1, 2, 3), 0, 8), ((4, 5, 6, 7), 0, 9)),
            [*ffn_pieces, *seeds, grad_pre, act],
        )
        moving.append(Moving(grid, parts))
        if first:
            moving[0].across()
    near_part = (back_kept[steps:] + came[steps:].astype(f32)).astype(bf16)
    near_part = grid.near_swap(near_part)

    grad_input, grad_blend, row_sums = call(
        blend_grad_kernel,
        "blend_backward",
        [
            ((steps, width), f32),
            ((steps, 2 * width), bf16),
            ((3, width), f32),
        ],
        [
            place,
            row_in,
            row_seed,
            back_kept,
            came,
            near_part,
            hidden_pre,
            update,
            hat,
            post_scale,
            line_of(later_normalizer_gain),
            spread,
        ],
        1,
    )
    (m_a, m_b) = moving
    m_a.value, m_b.parts, grad_blend = tie((m_a.value, m_b.parts, grad_blend))
    m_a.along()
    m_b.across()
    hidden_pieces = group(grad_blend)
    down = gathered(down_kept, down_sent)

    held = (m_a.value, m_b.value, hidden_pieces)
    m_a.value, m_b.value, hidden_pieces = tie(held)
    m_b.along()

    grad_reset, grad_value, probs_kept, probs_sent, span_sums = call(
        attention_grad_kernel,
        "attention_backward",
        [
            ((tokens, span), bf16),
            ((tokens, span), bf16),
            ((2 * steps, SPAN), f32),
            ((2 * steps, SPAN), f32),
            ((2, span), f32),
        ],
        [*hidden_pieces, reset_pre, attended, value, value_pre, probs_low, *w_second],
    )
    parts = weight_grad(
        grid,
        "reset_weights",
        width,
        (((0, 1, 2, 3), 0, 8), ((4, 5, 6, 7), 0, 9)),
        [*pieces, *hidden_pieces, grad_reset, mixed],
    )
    moving.append(Moving(grid, parts))
    m_c = moving[2]
    m_c.across()
    probs_gathered = gathered(probs_kept, probs_sent, f32)
    grad_gates, in_kept, *in_sent = call(
        functools.partial(input_grad_kernel, blocks),
        "input_backward",
        [((tokens, half), bf16), ((2 * steps, 2 * width), f32)]
        + [((2 * steps, half), bf16)] * 4,
        [place, *hidden_pieces, grad_reset, grad_value, spread, *w_first, *w_second],
        1,
    )
    m_b.value, in_kept, in_sent, down = tie((m_b.value, in_kept, in_sent, down))
    in_came = [swap(p) for p in in_sent]
    in_near = in_kept[steps:] + jnp.concatenate([p[steps:] for p in in_came], axis=1).astype(f32)
    in_near = grid.near_swap(in_near.astype(bf16))
    in_gathered = [in_kept, *in_came, in_near]
    grad_shared, narrow = call(
        score_grad_kernel,
        "scores_backward",
        [((steps, LANES), bf16), ((4, LANES), f32)],
        [*probs_gathered, probs, query, key, shared_pre, line_of(asking_gain), line_of(lookup_gain)],
    )
    parts = weight_grad(
        grid,
        "value_weights",
        width,
        (((0, 1, 2, 3), width, 4), ((0, 1, 2, 3), 0, 5), ((0,), 0, 6)),
        [*pieces, grad_value, grad_gates, grad_shared],
    )
    moving.append(Moving(grid, parts))
    m_d = moving[3]
    held = (m_c.value, m_d.parts, m_a.value, in_gathered)
    m_c.value, m_d.parts, m_a.value, in_gathered = tie(held)
    m_c.along()
    m_d.across()
    averages = call(
        ema_backward_kernel,
        "average_backward",
        [
            ((steps, width), bf16),
            ((steps, width), bf16),
            ((states + 8, width), f32),
            ((states + 8, width), f32),
        ],
        [
            place,
            row_in,
            gain,
            direct,
            params,
            spread,
            table,
            normed,
            pre,
            *in_gathered,
            grad_shared,
            grad_input,
            row_sums,
            seed_sum,
            narrow,
            *down,
            blended,
            line_of(outward_layer_offset),
            *w_first,
        ],
        1,
        [
            pltpu.VMEM((steps, width), f32),
            pltpu.VMEM((steps, width), f32),
            pltpu.VMEM((steps, width // LANES, LANES), f32),
        ],
    )
    sides = [m_a.near(), m_b.near()]
    held = (m_c.value, m_d.value, averages, sides)
    m_c.value, m_d.value, averages, sides = tie(held)
    m_d.along()
    grad_row, out_row, keep_rows, send_rows = averages

    lanes = COMMON_SPAN_DIM
    keep_rows = keep_rows + swap(send_rows)
    kept = keep_rows.shape[0]

    def placed(value):
        return near_order(value, jnp.zeros_like(value), 0).reshape(-1, width)

    wide_sums = [
        placed(span_sums[0]),
        placed(span_sums[1]),
        placed(jnp.concatenate(bffnin)),
    ]
    small = jnp.concatenate([keep_rows] + wide_sums, axis=0)
    sums = grid.sum_all(small)
    first_rows = sums[:kept]
    whole = in_order(first_rows, swap(sums)[:kept], 0)
    wide = sums[kept:]
    zero = whole[:states].T
    first = whole[kept : kept + states].T
    rate = jax.nn.sigmoid(inflow_logits)
    damp = jax.nn.sigmoid(decay_logits)
    grad_collapse = rate * channel_lifting * zero
    grad_inflow = channel_collapse * zero
    grad_keep = channel_collapse * rate * channel_lifting * first
    grad_lifting = grad_inflow * rate
    grad_rate = (grad_inflow * channel_lifting - grad_keep * damp) * rate * (1.0 - rate)
    grad_damp = -grad_keep * rate * damp * (1.0 - damp)
    rest = whole[states:]
    thin = rest[6].reshape(-1, lanes)

    (own_a, near_a), (own_b, near_b) = sides
    own_c, near_c = m_c.near()
    own_d, near_value, near_d = m_d.near((span,))
    out_in = near_order(
        jnp.concatenate([own_a[:, :ff], own_b[:, :ff]], axis=1),
        jnp.concatenate([near_a[:, :ff], near_b[:, :ff]], axis=1),
        1,
    )
    out_down = near_order(
        jnp.concatenate([own_a[:, ff:], own_b[:, ff:]], axis=1),
        jnp.concatenate([near_a[:, ff:], near_b[:, ff:]], axis=1),
        1,
    )
    out_reset = near_order(own_c[:, :span], near_c[:, :span], 1)
    out_wout = near_order(own_c[:, span:], near_c[:, span:], 1)
    out_value = near_order(own_d[:, :span], near_value, 1)
    own_d = own_d[:, span:]
    update_half = near_order(own_d[:, :quarter], near_d[:, :quarter], 1)
    hidden_half = near_order(own_d[:, quarter:half], near_d[:, quarter:half], 1)
    shared_half = own_d[:, half:] + near_d[:, half:]
    out_update = in_order(update_half, swap(update_half), 1)
    out_hidden = in_order(hidden_half, swap(hidden_half), 1)
    out_shared = shared_half + swap(shared_half)

    rows_out = jnp.stack([out_row, grad_row])
    rows_other = swap(rows_out)
    outputs = in_order(rows_out[:1], rows_other[:1], 0)
    grad_tokens = in_order(rows_out[1:], rows_other[1:], 0)
    return (
        outputs,
        grad_tokens,
        rest[0],
        grad_rate,
        grad_damp,
        grad_lifting,
        grad_collapse,
        rest[1],
        out_value,
        wide[0],
        out_shared,
        thin[0],
        thin[1],
        thin[2],
        thin[3],
        out_reset,
        wide[1],
        out_update,
        rest[2],
        out_hidden,
        rest[3],
        out_wout.T,
        rest[4],
        out_in,
        wide[2:].reshape(-1),
        out_down.T,
        rest[5],
    )


def solution(mesh):
    grid = Grid(mesh.shape["dp"])
    return jax.shard_map(
        functools.partial(per_device, grid),
        mesh=mesh,
        in_specs=(
            P(None, "dp", None),
            P(None, "dp", None),
            P(None, "dp"),
            P(),
            P(),
            P(),
            P(),
            P(),
            P(),
            P("dp", "mp"),
            P("mp"),
            P("dp", None),
            P(),
            P(),
            P(),
            P(),
            P("dp", "mp"),
            P("mp"),
            P("dp", None),
            P(),
            P("dp", None),
            P(),
            P("mp", "dp"),
            P(),
            P("dp", "mp"),
            P("mp"),
            P("mp", "dp"),
            P(),
        ),
        out_specs=(
            P(None, "dp", None),
            P(None, "dp", None),
            P(),
            P(),
            P(),
            P(),
            P(),
            P(),
            P("dp", "mp"),
            P("mp"),
            P("dp", None),
            P(),
            P(),
            P(),
            P(),
            P("dp", "mp"),
            P("mp"),
            P("dp", None),
            P(),
            P("dp", None),
            P(),
            P("mp", "dp"),
            P(),
            P("dp", "mp"),
            P("mp"),
            P("mp", "dp"),
            P(),
        ),
        check_vma=False,
    )
```
